128 devices in a mesh: member: 8 (over z, core), band: 16 (over x, y).
Axes of the slice: x: 4, y: 4, z: 4, core: 2. Of those that a mesh axis runs over, the one named last changes fastest.
Arguments:
- latent: bfloat16 [8, 4096, 1024], P('member', 'band'), may hold values from -6 to 6
- observed: bfloat16 [4096, 128], P('band'), may hold values from -6 to 6
- area_weight: float32 [4096], P('band'), may hold values from 0.3 to 25, as said below
- band_counts: int32 [16], replicated, may hold values from 128 to 256, as said below
- gain_attn: float32 [1024], replicated, may hold values from 0.25 to 1.75
- w_query: bfloat16 [1024, 1024], replicated, may hold values from -0.1875 to 0.1875
- w_key: bfloat16 [1024, 1024], replicated, may hold values from -0.1875 to 0.1875
- w_value: bfloat16 [1024, 1024], replicated, may hold values from -0.1875 to 0.1875
- w_out: bfloat16 [1024, 1024], replicated, may hold values from -1.5 to 1.5
- gain_head: float32 [1024], replicated, may hold values from 0.25 to 1.75
- w_head: bfloat16 [1024, 128], replicated, may hold values from -0.1875 to 0.1875
Outputs:
- grad_latent: bfloat16 [8, 4096, 1024], P('member', 'band')
- grad_head: float32 [1024, 128], P('band')
- ensemble_loss: float32 [], replicated
The draws below stay inside these ranges and needn't reach their ends.
Inputs may be any that keep to these rules, and one draw needn't show every extreme that they name: Band b holds band_counts[b] live grid points in its first slots; the remaining of its 256 slots are padding. In every draw some band holds exactly 256 and another exactly 128. `area_weight`: positive area weights.
All inputs are finite; a program needn't handle non-finite values.
Results may differ from the reference program's by a relative error of at most 0.019.
Values may be sent and summed in bfloat16 or wider, within the bound.
No kernel may reach another device: no remote copies, remote signals or barrier semaphores. Data moves between devices by JAX's collectives and lax.ppermute only.
A program may use at most 192 MiB of HBM per device.

```python
import math
import jax
import jax.numpy as jnp
from jax import lax

D = 1024
HEADS = 16
CH = 128
R = 512
CAP = 256
CMIN = 128
HOPS = 4
MEMBERS = 8
BANDS = 16
POINTS = 4096


def draw_band_counts(key, part):
    base_key = jax.random.fold_in(key, 11)
    first_key, order_key = jax.random.split(base_key)
    counts_drawn = jax.random.randint(first_key, (BANDS,), CMIN, CAP + 1)
    order_drawn = jax.random.permutation(order_key, BANDS)
    counts_drawn = counts_drawn.at[order_drawn[0]].set(CAP)
    counts_drawn = counts_drawn.at[order_drawn[1]].set(CMIN)
    return counts_drawn.astype(jnp.int32)


def draw_area_weight(key, part):
    noise_key = jax.random.fold_in(key, 23)
    band_place = (jnp.arange(POINTS) // CAP).astype(jnp.float32) / (BANDS - 1)
    rising = jnp.log(3.0)
    spread = 0.7
    rough = jax.random.uniform(noise_key, (POINTS,), jnp.float32, -spread, spread)
    return jnp.exp(rising * band_place + rough).astype(jnp.float32)


def level_of(rng, dims, pieces, least, top_value):
    def one(dim, shards_of):
        draws = jax.random.uniform(jax.random.fold_in(jax.random.fold_in(rng, 6), dim), (shards_of,), jnp.float32, least / len(pieces), top_value / len(pieces))
        return jnp.repeat(jnp.exp(draws), dims[dim] // shards_of).reshape((-1,) + (1,) * (len(dims) - dim - 1))

    factor_of = one(*pieces[0])
    for cut in pieces[1:]:
        factor_of = factor_of * one(*cut)
    return factor_of


def noise(own_key, shape, scale, most, shards=(), kind=jnp.bfloat16):
    values = scale * jax.random.normal(own_key, shape, jnp.float32)
    if shards:
        values = values * level_of(own_key, shape, shards, -0.22, 0.18)
    return jnp.clip(values, -most, most).astype(kind)


def setup_inputs(seed: int = 0) -> dict:
    key_list = jax.random.split(jax.random.key(seed), 12)
    latent = noise(key_list[0], (MEMBERS, POINTS, D), 1.0, 6.0, ((0, 8), (1, 16)))
    observed = noise(key_list[1], (POINTS, CH), 1.0, 6.0, ((0, 16),))
    area_weight = draw_area_weight(jax.random.fold_in(key_list[11], 71), 0)
    band_counts = draw_band_counts(jax.random.fold_in(key_list[11], 71), 0)
    gain_attn = jnp.clip(1.0 + 0.15 * jax.random.normal(key_list[4], (D,), jnp.float32), 0.25, 1.75)
    w_query = noise(key_list[5], (D, D), D ** -0.5, 0.1875)
    w_key = noise(key_list[6], (D, D), D ** -0.5, 0.1875)
    w_value = noise(key_list[7], (D, D), D ** -0.5, 0.1875)
    w_out = noise(key_list[8], (D, D), (D // 64) ** -0.5, 1.5)
    gain_head = jnp.clip(1.0 + 0.15 * jax.random.normal(key_list[9], (D,), jnp.float32), 0.25, 1.75)
    w_head = noise(key_list[10], (D, CH), D ** -0.5, 0.1875)
    return dict(latent=latent, observed=observed, area_weight=area_weight, band_counts=band_counts, gain_attn=gain_attn, w_query=w_query, w_key=w_key, w_value=w_value, w_out=w_out, gain_head=gain_head, w_head=w_head)


NORM_EPS = 1e-06
SMOOTH_WIDTH = 0.25
FAIR_ALPHA = 0.95
heads_per_group = 4

def inverse_rms(values):
    return lax.rsqrt(lax.optimization_barrier(jnp.mean(values * values, axis=-1, keepdims=True)) + NORM_EPS)

def norm_backward(values, gain_vec, inverse, upstream):
    scaled = upstream * gain_vec
    return inverse * scaled - values * inverse ** 3 * lax.optimization_barrier(jnp.mean(values * scaled, axis=-1, keepdims=True))

def times_transposed(left_side, scaling_coefficient):
    return lax.dot_general(left_side, scaling_coefficient, (((left_side.ndim - 1,), (1,)), ((), ())), preferred_element_type=jnp.float32)

def window_probs(query_group, key_group, allowed):
    head_size = query_group.shape[-1]
    scores = jnp.einsum('mqgd,mkgd->mgqk', query_group.astype(jnp.float32), key_group.astype(jnp.float32)) / math.sqrt(head_size)
    exponent = jnp.where(allowed[None, None], jnp.exp(scores), 0.0)
    return exponent / lax.optimization_barrier(jnp.sum(exponent, axis=-1, keepdims=True))

def split_group(array_in, first_col, group_width, head_size):
    part_cols = lax.dynamic_slice_in_dim(array_in, first_col, group_width, 2)
    return part_cols.reshape(array_in.shape[0], array_in.shape[1], heads_per_group, head_size)

def attention_forward(queries, key_rows, value_rows, allowed):
    number_of_realizations, row_count, model_width = queries.shape
    head_size = model_width // HEADS
    group_width = heads_per_group * head_size

    def one_group(group_index, output):
        first_col = (group_index * group_width).astype(jnp.int32)
        query_group = split_group(queries, first_col, group_width, head_size)
        key_group = split_group(key_rows, first_col, group_width, head_size)
        value_group = split_group(value_rows, first_col, group_width, head_size)
        soft_b = window_probs(query_group, key_group, allowed).astype(jnp.bfloat16)
        mixed_group = jnp.einsum('mgqk,mkgd->mqgd', soft_b.astype(jnp.float32), value_group.astype(jnp.float32))
        mixed_group = mixed_group.reshape(number_of_realizations, row_count, group_width).astype(jnp.bfloat16)
        return lax.dynamic_update_slice_in_dim(output, mixed_group, first_col, 2)
    return lax.fori_loop(0, model_width // group_width, one_group, jnp.zeros(queries.shape, jnp.bfloat16))

def attention_backward(queries, key_rows, value_rows, allowed, grad_mixed):
    number_of_realizations, row_count, model_width = queries.shape
    key_count = key_rows.shape[1]
    head_size = model_width // HEADS
    group_width = heads_per_group * head_size
    score_scale = 1.0 / math.sqrt(head_size)

    def one_group(group_index, carried):
        grad_query, grad_key, grad_value = carried
        first_col = (group_index * group_width).astype(jnp.int32)
        query_group = split_group(queries, first_col, group_width, head_size)
        key_group = split_group(key_rows, first_col, group_width, head_size)
        value_group = split_group(value_rows, first_col, group_width, head_size)
        upstream_group = split_group(grad_mixed, first_col, group_width, head_size)
        soft = window_probs(query_group, key_group, allowed)
        soft_b = soft.astype(jnp.bfloat16)
        d_soft = jnp.einsum('mqgd,mkgd->mgqk', upstream_group.astype(jnp.float32), value_group.astype(jnp.float32))
        inner_sum = lax.optimization_barrier(jnp.sum(soft * d_soft, axis=-1, keepdims=True))
        d_score = (soft * (d_soft - inner_sum) * score_scale).astype(jnp.bfloat16)
        query_part = jnp.einsum('mgqk,mkgd->mqgd', d_score.astype(jnp.float32), key_group.astype(jnp.float32))
        key_part = jnp.einsum('mgqk,mqgd->mkgd', d_score.astype(jnp.float32), query_group.astype(jnp.float32))
        value_part = jnp.einsum('mgqk,mqgd->mkgd', soft_b.astype(jnp.float32), upstream_group.astype(jnp.float32))
        grad_query = lax.dynamic_update_slice_in_dim(grad_query, query_part.reshape(number_of_realizations, row_count, group_width).astype(jnp.bfloat16), first_col, 2)
        grad_key = lax.dynamic_update_slice_in_dim(grad_key, key_part.reshape(number_of_realizations, key_count, group_width).astype(jnp.bfloat16), first_col, 2)
        grad_value = lax.dynamic_update_slice_in_dim(grad_value, value_part.reshape(number_of_realizations, key_count, group_width).astype(jnp.bfloat16), first_col, 2)
        return (grad_query, grad_key, grad_value)
    initial = (jnp.zeros(queries.shape, jnp.bfloat16), jnp.zeros(key_rows.shape, jnp.bfloat16), jnp.zeros(value_rows.shape, jnp.bfloat16))
    return lax.fori_loop(0, model_width // group_width, one_group, initial)

def probabilistic_accuracy(predicted_states, measured_part, scaling_coefficient):
    number_of_realizations = predicted_states.shape[0]
    fair_factor = 1.0 - (1.0 - FAIR_ALPHA) / number_of_realizations
    gap_from_measured = predicted_states - measured_part[None]
    smooth_observed = jnp.sqrt(gap_from_measured * gap_from_measured + SMOOTH_WIDTH * SMOOTH_WIDTH)
    between_realization_gap = predicted_states[:, None] - predicted_states[None, :]
    smooth_pair = jnp.sqrt(between_realization_gap * between_realization_gap + SMOOTH_WIDTH * SMOOTH_WIDTH)
    off_diagonal = (1.0 - jnp.eye(number_of_realizations, dtype=jnp.float32))[:, :, None, None]
    point_score = lax.optimization_barrier(jnp.sum(smooth_observed, axis=0)) / number_of_realizations - fair_factor / (2.0 * number_of_realizations * (number_of_realizations - 1)) * lax.optimization_barrier(jnp.sum(off_diagonal * smooth_pair, axis=(0, 1)))
    total = jnp.sum(scaling_coefficient[:, None] * point_score)
    gradient = scaling_coefficient[None, :, None] * (gap_from_measured / smooth_observed / number_of_realizations - fair_factor / (number_of_realizations * (number_of_realizations - 1.0)) * lax.optimization_barrier(jnp.sum(between_realization_gap / smooth_pair, axis=1)))
    return (total, gradient)

def reference(latent, observed, area_weight, band_counts, gain_attn, w_query, w_key, w_value, w_out, gain_head, w_head):
    number_of_realizations = latent.shape[0]
    window_rows = (2 * HOPS + 1) * CAP
    pad_rows = HOPS * CAP
    slot_iota = jnp.arange(CAP, dtype=jnp.int32)
    offsets = (jnp.cumsum(band_counts) - band_counts).astype(jnp.int32)
    positions = (offsets[:, None] + slot_iota[None, :]).reshape(-1).astype(jnp.int32)
    live = (slot_iota[None, :] < band_counts[:, None]).reshape(-1)
    pos_pad = jnp.concatenate([jnp.zeros((pad_rows,), jnp.int32), positions, jnp.zeros((pad_rows,), jnp.int32)])
    live_pad = jnp.concatenate([jnp.zeros((pad_rows,), bool), live, jnp.zeros((pad_rows,), bool)])
    latent_f = latent.astype(jnp.float32)
    inverse_one = inverse_rms(latent_f)
    normed = (latent_f * inverse_one * gain_attn).astype(jnp.bfloat16)
    queries = jnp.dot(normed, w_query, preferred_element_type=jnp.float32).astype(jnp.bfloat16)
    key_rows = jnp.dot(normed, w_key, preferred_element_type=jnp.float32).astype(jnp.bfloat16)
    value_rows = jnp.dot(normed, w_value, preferred_element_type=jnp.float32).astype(jnp.bfloat16)
    zero_pad = jnp.zeros((number_of_realizations, pad_rows, D), jnp.bfloat16)
    key_pad = jnp.concatenate([zero_pad, key_rows, zero_pad], axis=1)
    value_pad = jnp.concatenate([zero_pad, value_rows, zero_pad], axis=1)

    def band_window(band_index):
        first_row = (band_index * CAP).astype(jnp.int32)
        query_block = lax.dynamic_slice_in_dim(queries, first_row, CAP, 1)
        key_block = lax.dynamic_slice_in_dim(key_pad, first_row, window_rows, 1)
        value_block = lax.dynamic_slice_in_dim(value_pad, first_row, window_rows, 1)
        query_pos = lax.dynamic_slice_in_dim(positions, first_row, CAP, 0)
        key_pos = lax.dynamic_slice_in_dim(pos_pad, first_row, window_rows, 0)
        key_live = lax.dynamic_slice_in_dim(live_pad, first_row, window_rows, 0)
        allowed = key_live[None, :] & (jnp.abs(query_pos[:, None] - key_pos[None, :]) <= R)
        return (first_row, query_block, key_block, value_block, allowed)

    def band_forward(band_index):
        window = band_window(band_index)
        return attention_forward(window[1], window[2], window[3], window[4])
    band_list = jnp.arange(BANDS, dtype=jnp.int32)
    mixed_blocks = lax.map(band_forward, band_list)
    mixed_out = jnp.transpose(mixed_blocks, (1, 0, 2, 3)).reshape(number_of_realizations, POINTS, D)
    hidden = latent_f + jnp.dot(mixed_out, w_out, preferred_element_type=jnp.float32)
    inverse_two = inverse_rms(hidden)
    head_in = (hidden * inverse_two * gain_head).astype(jnp.bfloat16)
    predicted = jnp.dot(head_in, w_head, preferred_element_type=jnp.float32).astype(jnp.bfloat16)
    point_weight = area_weight * live.astype(jnp.float32) / (jnp.sum(band_counts).astype(jnp.float32) * CH)
    ensemble_loss, gradient = probabilistic_accuracy(predicted.astype(jnp.float32), observed.astype(jnp.float32), point_weight)
    grad_pred = gradient.astype(jnp.bfloat16)
    grad_head = lax.dot_general(head_in.reshape(-1, D), grad_pred.reshape(-1, CH), (((0,), (0,)), ((), ())), preferred_element_type=jnp.float32)
    grad_hidden = norm_backward(hidden, gain_head, inverse_two, times_transposed(grad_pred, w_head))
    grad_mixed = times_transposed(grad_hidden.astype(jnp.bfloat16), w_out).astype(jnp.bfloat16)

    def band_backward(normed_acc, band_index):
        window = band_window(band_index)
        first_row = window[0]
        upstream = lax.dynamic_slice_in_dim(grad_mixed, first_row, CAP, 1)
        grad_query, key_term, value_term = attention_backward(window[1], window[2], window[3], window[4], upstream)
        normed_term = (times_transposed(key_term, w_key) + times_transposed(value_term, w_value)).astype(jnp.bfloat16)
        normed_sum = lax.dynamic_slice_in_dim(normed_acc, first_row, window_rows, 1) + normed_term.astype(jnp.float32)
        normed_acc = lax.dynamic_update_slice_in_dim(normed_acc, normed_sum, first_row, 1)
        return (normed_acc, grad_query)
    acc_zero = jnp.zeros((number_of_realizations, POINTS + 2 * pad_rows, D), jnp.float32)
    normed_acc, query_blocks = lax.scan(band_backward, acc_zero, band_list)
    grad_queries = jnp.transpose(query_blocks, (1, 0, 2, 3)).reshape(number_of_realizations, POINTS, D)
    grad_normed = times_transposed(grad_queries, w_query) + normed_acc[:, pad_rows:pad_rows + POINTS]
    grad_latent = (grad_hidden + norm_backward(latent_f, gain_attn, inverse_one, grad_normed)).astype(jnp.bfloat16)
    return (grad_latent, grad_head, ensemble_loss)
```

```python
import jax
import jax.numpy as jnp
from jax import lax
from jax.experimental import pallas as pl
from jax.experimental.pallas import tpu as pltpu
from jax.sharding import PartitionSpec as P

HEADS = 16
HEAD = 64
CH = 128
R = 512
CAP = 256
MEMBERS = 8
BANDS = 16
EPS = 1e-06
SMOOTH = 0.0625
FAIR = 1.0 - 0.05 / MEMBERS
PAIR_SCALE = FAIR / (MEMBERS * (MEMBERS - 1.0))

WIDTH = 2 * R + CAP + 128
ROWS = BANDS * CAP - CAP + WIDTH
EDGE = 384
CHUNKS = ((0, EDGE, 1), (EDGE, 2 * R, 0), (2 * R, WIDTH, 2))
HEAD_ROWS = 64
SENT_ROWS = 128 + HEAD_ROWS + 16

f32 = jnp.float32
bf16 = jnp.bfloat16


def dot(a, b):
    return lax.dot_general(a, b, (((1,), (0,)), ((), ())), preferred_element_type=f32)


def dot_nt(a, b):
    return lax.dot_general(a, b, (((1,), (1,)), ((), ())), preferred_element_type=f32)


def dot_tn(a, b):
    return lax.dot_general(a, b, (((0,), (0,)), ((), ())), preferred_element_type=f32)


def swap(x):
    return pltpu.roll(x, HEAD, axis=1)


def low_lanes(rows):
    return lax.broadcasted_iota(jnp.int32, (rows, 128), 1) < HEAD


def store_halves(pair, write):
    low = low_lanes(128)
    top, bottom = pair[:128], pair[128:]
    write(0, jnp.where(low, top, swap(bottom)).astype(bf16))
    write(1, jnp.where(low, swap(top), bottom).astype(bf16))


def load_halves(first, second):
    low = low_lanes(128)
    first, second = first.astype(f32), second.astype(f32)
    top = jnp.where(low, first, swap(second))
    bottom = jnp.where(low, swap(first), second)
    return top.astype(bf16), bottom.astype(bf16)


def project_kernel(lat_ref, gain_ref, wq_ref, wk_ref, wv_ref, out_ref):
    x = lat_ref[...].astype(f32)
    inverse = lax.rsqrt(jnp.mean(x * x, axis=-1, keepdims=True) + EPS)
    normed = (x * inverse * gain_ref[...]).astype(bf16)
    low = low_lanes(CAP)
    for quad in range(4):
        cols = slice(quad * 256, quad * 256 + 256)
        q = dot(normed, wq_ref[:, cols]) * 0.125
        k = dot(normed, wk_ref[:, cols])
        v = dot(normed, wv_ref[:, cols])
        for half in range(2):
            head = quad * 4 + half * 2
            part = slice(half * 128, half * 128 + 128)

            def write(i, value):
                out_ref[head + i, 0:128, :] = value

            store_halves(q[:, part], write)
            kp, vp = k[:, part], v[:, part]
            out_ref[head, 128:384, :] = jnp.where(low, kp, swap(vp)).astype(bf16)
            out_ref[head + 1, 128:384, :] = jnp.where(low, swap(kp), vp).astype(bf16)


def query_rows(packed):
    low = low_lanes(128)
    zero = jnp.zeros((128, 128), f32)
    packed = packed.astype(f32)
    return jnp.concatenate(
        [jnp.where(low, packed, zero), jnp.where(low, swap(packed), zero)], 0
    ).astype(bf16)


def upstream_rows(packed):
    low = low_lanes(128)
    zero = jnp.zeros((128, 128), f32)
    packed = packed.astype(f32)
    return jnp.concatenate(
        [jnp.where(low, zero, swap(packed)), jnp.where(low, zero, packed)], 0
    ).astype(bf16)


def exponents(scores, bias, mode, rel):
    e = jnp.exp(scores + jnp.concatenate([bias, bias], 1))
    if mode:
        gap = lax.broadcasted_iota(jnp.int32, e.shape, 0) - lax.broadcasted_iota(
            jnp.int32, e.shape, 1
        )
        e = jnp.where(gap >= rel if mode == 1 else gap <= rel, e, 0.0)
    return e


def forward_kernel(
    counts_ref, x_ref, mixed_ref, exact_ref, inverse_ref, kv_ref, kt_ref, bias_ref, rows_ref, vt_ref
):
    rows_ref[...] = jnp.zeros((ROWS, 128), f32)
    sub = lax.broadcasted_iota(jnp.int32, (1, 8, 128), 1)
    row = lax.broadcasted_iota(jnp.int32, (CAP, 128), 0)

    def place(b, off):
        count = counts_ref[b]
        shift = off & 7
        base = pl.multiple_of(off - shift + R, 8)
        x = jnp.where(row < count, x_ref[b, 128:384, :].astype(f32), 0.0)
        turned = pltpu.roll(x.reshape(32, 8, 128), shift, axis=1)
        before = rows_ref[pl.ds(base, 8), :].reshape(1, 8, 128)
        shifted = jnp.concatenate([before, turned], 0)
        turned = jnp.concatenate([turned, jnp.zeros((1, 8, 128), f32)], 0)
        rows_ref[pl.ds(base, 264), :] = jnp.where(sub < shift, shifted, turned).reshape(264, 128)
        return off + count

    total = lax.fori_loop(0, BANDS, place, jnp.int32(0))
    vt_ref[HEAD:, :] = jnp.ones((16, ROWS), bf16)
    tile_row = lax.broadcasted_iota(jnp.int32, (128, 128), 0)
    for t in range(ROWS // 128):
        span = slice(t * 128, t * 128 + 128)
        tile = rows_ref[span, :]
        kv_ref[span, :] = tile.astype(bf16)
        turned = tile.T
        kt_ref[:, span] = turned[:HEAD].astype(bf16)
        vt_ref[:HEAD, span] = turned[HEAD:].astype(bf16)
        position = tile_row + (t * 128 - R)
        bias_ref[span, :] = jnp.where((position >= 0) & (position < total), 0.0, -1e30)

    def band(b, off):
        rel = off & 127
        start = pl.multiple_of(off - rel, 128)
        q = query_rows(x_ref[b, 0:128, :])
        out = jnp.zeros((HEAD + 16, CAP), f32)
        for first, last, mode in CHUNKS:
            span = pl.ds(pl.multiple_of(start + first, 128), last - first)
            s = dot_nt(kv_ref[span, :], q)
            e = exponents(s, bias_ref[span, :], mode, rel).astype(bf16)
            out = out + dot(vt_ref[:, span], e)
        inverse = 1.0 / out[HEAD : HEAD + 1, :]
        inverse_ref[pl.ds(b, 1), :] = inverse
        out = out[:HEAD] * inverse
        mixed = jnp.concatenate([out[:, :128], out[:, 128:]], 0).T
        exact_ref[b] = mixed
        mixed_ref[b] = mixed.astype(bf16)
        return off + counts_ref[b]

    lax.fori_loop(0, BANDS, band, jnp.int32(0))


def head_kernel(mixed_ref, lat_ref, wo_ref, gain_ref, wh_ref, hidden_ref, pred_ref, rows_ref):
    for pair in range(8):
        top, bottom = load_halves(mixed_ref[2 * pair], mixed_ref[2 * pair + 1])
        rows_ref[:128, pair * 128 : pair * 128 + 128] = top
        rows_ref[128:, pair * 128 : pair * 128 + 128] = bottom
    hidden = lat_ref[...].astype(f32) + dot(rows_ref[...], wo_ref[...])
    hidden_ref[...] = hidden
    inverse = lax.rsqrt(jnp.mean(hidden * hidden, axis=-1, keepdims=True) + EPS)
    head_in = (hidden * inverse * gain_ref[...]).astype(bf16)
    predicted = dot(head_in, wh_ref[...]).astype(bf16)
    for j in range(MEMBERS):
        pred_ref[j] = predicted


def split3(x):
    high = x.astype(bf16)
    rest = x - high.astype(f32)
    middle = rest.astype(bf16)
    low = (rest - middle.astype(f32)).astype(bf16)
    return high, middle, low


def loss_kernel(
    place_ref, counts_ref, pred_ref, obs_ref, area_ref, hidden_ref, gain_ref, wh_ref, wo_ref,
    grad_ref, out_ref,
):
    me, band = place_ref[0], place_ref[1]
    total = lax.fori_loop(0, BANDS, lambda b, t: t + counts_ref[b], jnp.int32(0))
    area = area_ref[...]
    weight = jnp.concatenate(
        [jnp.broadcast_to(area[i : i + 1, :], (128, 128)).T for i in range(2)], 0
    )
    row = lax.broadcasted_iota(jnp.int32, (CAP, CH), 0)
    weight = jnp.where(row < counts_ref[band], weight, 0.0) / (total.astype(f32) * CH)
    mine = pred_ref[me].astype(f32)

    def smooth(gap):
        square = gap * gap + SMOOTH
        inverse = lax.rsqrt(square)
        return square * inverse, gap * inverse

    size, slope = smooth(mine - obs_ref[...].astype(f32))
    pair_size = jnp.zeros((CAP, CH), f32)
    pair_slope = jnp.zeros((CAP, CH), f32)
    for k in range(MEMBERS):
        a, da = smooth(mine - pred_ref[k].astype(f32))
        pair_size = pair_size + jnp.where(me == k, 0.0, 1.0) * a
        pair_slope = pair_slope + da
    loss = jnp.sum(weight * (size / MEMBERS - (0.5 * PAIR_SCALE) * pair_size), axis=0, keepdims=True)
    grad_pred = (weight * (slope / MEMBERS - PAIR_SCALE * pair_slope)).astype(bf16)

    hidden = hidden_ref[...]
    gain = gain_ref[...]
    inverse = lax.rsqrt(jnp.mean(hidden * hidden, axis=-1, keepdims=True) + EPS)
    head_in = (hidden * inverse * gain).astype(bf16)
    grad_head = dot_tn(head_in, grad_pred).astype(bf16)
    scaled = dot_nt(grad_pred, wh_ref[...]) * gain
    grad_hidden = inverse * scaled - hidden * (inverse * inverse * inverse) * jnp.mean(
        hidden * scaled, axis=-1, keepdims=True
    )
    grad_ref[...] = grad_hidden
    grad_mixed = dot_nt(grad_hidden.astype(bf16), wo_ref[...])
    pieces = [jnp.broadcast_to(p, (1, 128)).astype(f32) for p in split3(loss)]
    pieces = jnp.concatenate(pieces + [jnp.zeros((13, 128), f32)], 0).astype(bf16)
    for pair in range(8):

        def write(i, value):
            out_ref[2 * pair + i, 0:128, :] = value

        store_halves(grad_mixed[:, pair * 128 : pair * 128 + 128], write)
    for b in range(BANDS):
        out_ref[b, 128:192, :] = grad_head[b * HEAD_ROWS : (b + 1) * HEAD_ROWS]
        out_ref[b, 192:208, :] = pieces


def share_kernel(sent_ref, out_ref):
    grad = jnp.zeros((HEAD_ROWS, CH), f32)
    loss = jnp.zeros((16, 128), f32)
    for b in range(BANDS):
        grad = grad + sent_ref[b, 128:192, :].astype(f32)
        loss = loss + sent_ref[b, 192:208, :].astype(f32)
    loss = jnp.sum(loss, axis=0, keepdims=True)
    pieces = jnp.concatenate(
        [p.astype(f32) for p in split3(loss)] + [jnp.zeros((13, 128), f32)], 0
    ).astype(bf16)
    grad = grad.astype(bf16)
    for j in range(MEMBERS):
        out_ref[j, :HEAD_ROWS, :] = grad
        out_ref[j, HEAD_ROWS:, :] = pieces


def total_kernel(shared_ref, grad_ref, loss_ref):
    grad = jnp.zeros((HEAD_ROWS, CH), f32)
    loss = jnp.zeros((16, 128), f32)
    for j in range(MEMBERS):
        grad = grad + shared_ref[j, :HEAD_ROWS, :].astype(f32)
        loss = loss + shared_ref[j, HEAD_ROWS:, :].astype(f32)
    grad_ref[...] = grad
    loss_ref[...] = jnp.sum(jnp.sum(loss, axis=0, keepdims=True), axis=1, keepdims=True)


def backward_kernel(
    counts_ref, x_ref, sent_ref, exact_ref, inverse_ref, kv_ref, kt_ref, bias_ref, out_ref, acc_ref
):
    acc_ref[...] = jnp.zeros((ROWS, 128), f32)

    def band(b, off):
        rel = off & 127
        start = pl.multiple_of(off - rel, 128)
        q = query_rows(x_ref[b, 0:128, :])
        upstream = sent_ref[b, 0:128, :]
        g = upstream_rows(upstream)
        both = jnp.concatenate([q, g], 0)
        product = (exact_ref[b] * upstream.astype(f32)).T
        inner = jnp.concatenate(
            [
                jnp.sum(product[:HEAD], axis=0, keepdims=True),
                jnp.sum(product[HEAD:], axis=0, keepdims=True),
            ],
            1,
        )
        inverse = inverse_ref[pl.ds(b, 1), :]
        grad_q = jnp.zeros((HEAD, CAP), f32)
        for first, last, mode in CHUNKS:
            span = pl.ds(pl.multiple_of(start + first, 128), last - first)
            kv = kv_ref[span, :]
            p = exponents(dot_nt(kv, q), bias_ref[span, :], mode, rel) * inverse
            ds = (p * (dot_nt(kv, g) - inner)).astype(bf16)
            acc_ref[span, :] += dot(jnp.concatenate([ds, p.astype(bf16)], 1), both)
            grad_q = grad_q + dot(kt_ref[:, span], ds)
        grad_q = grad_q * 0.125
        out_ref[b, 0:128, :] = jnp.concatenate([grad_q[:, :128], grad_q[:, 128:]], 0).T.astype(bf16)
        return off + counts_ref[b]

    lax.fori_loop(0, BANDS, band, jnp.int32(0))
    sub = lax.broadcasted_iota(jnp.int32, (1, 8, 128), 1)
    row = lax.broadcasted_iota(jnp.int32, (CAP, 128), 0)

    def give(b, off):
        count = counts_ref[b]
        shift = off & 7
        base = pl.multiple_of(off - shift + R, 8)
        x = acc_ref[pl.ds(base, 264), :].reshape(33, 8, 128)
        turned = pltpu.roll(x, (8 - shift) & 7, axis=1)
        x = jnp.where(sub + shift < 8, turned[:32], turned[1:]).reshape(CAP, 128)
        out_ref[b, 128:384, :] = jnp.where(row < count, x, 0.0).astype(bf16)
        return off + count

    lax.fori_loop(0, BANDS, give, jnp.int32(0))


def latent_kernel(
    d_ref, lat_ref, gain_ref, wq_ref, wk_ref, wv_ref, grad_ref, out_ref, dq_ref, dk_ref, dv_ref
):
    low = low_lanes(CAP)
    for pair in range(8):
        cols = slice(pair * 128, pair * 128 + 128)
        top, bottom = load_halves(d_ref[2 * pair, 0:128, :], d_ref[2 * pair + 1, 0:128, :])
        dq_ref[:128, cols] = top
        dq_ref[128:, cols] = bottom
        first = d_ref[2 * pair, 128:384, :].astype(f32)
        second = d_ref[2 * pair + 1, 128:384, :].astype(f32)
        dk_ref[:, cols] = jnp.where(low, first, swap(second)).astype(bf16)
        dv_ref[:, cols] = jnp.where(low, swap(first), second).astype(bf16)
    normed = (
        dot_nt(dq_ref[...], wq_ref[...])
        + dot_nt(dk_ref[...], wk_ref[...])
        + dot_nt(dv_ref[...], wv_ref[...])
    )
    x = lat_ref[...].astype(f32)
    inverse = lax.rsqrt(jnp.mean(x * x, axis=-1, keepdims=True) + EPS)
    scaled = normed * gain_ref[...]
    out_ref[...] = (
        grad_ref[...]
        + inverse * scaled
        - x * (inverse * inverse * inverse) * jnp.mean(x * scaled, axis=-1, keepdims=True)
    ).astype(bf16)


def call(kernel, outs, scalars, arrays, scratch=(), name=None):
    vmem = pl.BlockSpec(memory_space=pltpu.VMEM)
    smem = pl.BlockSpec(memory_space=pltpu.SMEM)
    return pl.pallas_call(
        kernel,
        out_shape=tuple(jax.ShapeDtypeStruct(s, d) for s, d in outs),
        in_specs=[smem] * len(scalars) + [vmem] * len(arrays),
        out_specs=tuple(vmem for _ in outs),
        scratch_shapes=[pltpu.VMEM(s, d) for s, d in scratch],
        name=name,
    )(*scalars, *arrays)


def attend_forward(counts, x):
    return call(
        forward_kernel,
        [
            ((BANDS, 128, 128), bf16),
            ((BANDS, 128, 128), f32),
            ((BANDS, CAP), f32),
            ((ROWS, 128), bf16),
            ((HEAD, ROWS), bf16),
            ((ROWS, 128), f32),
        ],
        [counts],
        [x],
        [((ROWS, 128), f32), ((HEAD + 16, ROWS), bf16)],
        name="attend_forward",
    )


def attend_backward(counts, x, sent, exact, inverse, kv, kt, bias):
    return call(
        backward_kernel,
        [((BANDS, 384, 128), bf16)],
        [counts],
        [x, sent, exact, inverse, kv, kt, bias],
        [((ROWS, 128), f32)],
        name="attend_backward",
    )[0]


def exchange(x, axis):
    return lax.all_to_all(x, axis, split_axis=0, concat_axis=0, tiled=True)


def body(
    latent, observed, area_weight, counts, gain_attn, w_query, w_key, w_value, w_out, gain_head, w_head
):
    members, cap, width = latent.shape
    lat = latent.reshape(cap, width)
    gain_a = gain_attn.reshape(1, width)
    gain_h = gain_head.reshape(1, width)
    area = area_weight.reshape(2, 128)
    place = jnp.stack([lax.axis_index("member"), lax.axis_index("band")]).astype(jnp.int32)
    (sent,) = call(
        project_kernel,
        [((HEADS, 384, 128), bf16)],
        [],
        [lat, gain_a, w_query, w_key, w_value],
        name="project",
    )
    x = exchange(sent, "band")
    mixed, exact, inverse, kv, kt, bias = attend_forward(counts, x)
    mixed = exchange(mixed, "band")
    hidden, predicted = call(
        head_kernel,
        [((cap, width), f32), ((MEMBERS, cap, CH), bf16)],
        [],
        [mixed, lat, w_out, gain_h, w_head],
        [((cap, width), bf16)],
        name="head",
    )
    predicted = exchange(predicted, "member")
    grad_hidden, sent = call(
        loss_kernel,
        [((cap, width), f32), ((BANDS, SENT_ROWS, 128), bf16)],
        [place, counts],
        [predicted, observed, area, hidden, gain_h, w_head, w_out],
        name="loss",
    )
    sent = exchange(sent, "band")
    (shared,) = call(
        share_kernel, [((MEMBERS, HEAD_ROWS + 16, 128), bf16)], [], [sent], name="share"
    )
    shared = exchange(shared, "member")
    grads = attend_backward(counts, x, sent, exact, inverse, kv, kt, bias)
    grads = exchange(grads, "band")
    grad_head, loss = call(
        total_kernel, [((HEAD_ROWS, CH), f32), ((1, 1), f32)], [], [shared], name="total"
    )
    (grad_latent,) = call(
        latent_kernel,
        [((cap, width), bf16)],
        [],
        [grads, lat, gain_a, w_query, w_key, w_value, grad_hidden],
        [((cap, width), bf16)] * 3,
        name="latent",
    )
    return grad_latent.reshape(latent.shape), grad_head, loss.reshape(())


def solution(mesh):
    rows = P("member", "band", None)
    placed = (rows, P("band", None), P("band")) + (P(),) * 8
    return jax.shard_map(
        body,
        mesh=mesh,
        in_specs=placed,
        out_specs=(rows, P("band", None), P()),
        check_vma=False,
    )
```

```python
import functools

import jax
import jax.numpy as jnp
from jax import lax
from jax.experimental import pallas as pl
from jax.experimental.pallas import tpu as pltpu
from jax.sharding import PartitionSpec as P

HEADS = 16
HEAD = 64
CH = 128
R = 512
CAP = 256
MEMBERS = 8
BANDS = 16
LOG2E = 1.4426950408889634
EPS = 1e-06
SMOOTH = 0.0625
FAIR = 1.0 - 0.05 / MEMBERS
PAIR_SCALE = FAIR / (MEMBERS * (MEMBERS - 1.0))

HALF = CAP // 2
WIDTH = 2 * R + CAP + 128
COLS = BANDS * CAP - CAP + WIDTH
EDGE = CAP + 128
STEPS = ((0, 512), (512, 512), (1024, 384))
DEAD = -32768.0
ONES, BIAS, AGAIN, DEPTH = 128, 144, 192, 256
TURNED = 144
UNROLL = 2
HEAD_ROWS = 64

f32 = jnp.float32
bf16 = jnp.bfloat16


def dot(a, b):
    return lax.dot_general(a, b, (((1,), (0,)), ((), ())), preferred_element_type=f32)


def dot_nt(a, b):
    return lax.dot_general(a, b, (((1,), (1,)), ((), ())), preferred_element_type=f32)


def dot_tn(a, b):
    return lax.dot_general(a, b, (((0,), (0,)), ((), ())), preferred_element_type=f32)


def swap(x):
    return pltpu.roll(x, HEAD, axis=1)


def lanes(rows):
    return lax.broadcasted_iota(jnp.int32, (rows, 128), 1)


def low_lanes(rows):
    return lanes(rows) < HEAD


def fold(first, second):
    low = low_lanes(64)
    return jnp.where(low, first, swap(second)), jnp.where(low, swap(first), second)


def unfold(packed):
    packed = packed.astype(f32)
    other = swap(packed)
    return jnp.concatenate([packed[:64], other[:64], packed[64:], other[64:]], 0)


def refold(rows):
    low = low_lanes(64)
    return jnp.concatenate(
        [jnp.where(low, rows[i : i + 64], swap(rows[i + 64 : i + 128])) for i in (0, 128)], 0
    )


def split3(x):
    high = x.astype(bf16).astype(f32)
    middle = (x - high).astype(bf16).astype(f32)
    return high, middle, (x - high - middle).astype(bf16).astype(f32)


def inverse_rms(x):
    return lax.rsqrt(jnp.mean(x * x, axis=-1, keepdims=True) + EPS)


def norm_backward(x, inverse, scaled):
    return inverse * scaled - x * (inverse * inverse * inverse) * jnp.mean(
        x * scaled, axis=-1, keepdims=True
    )


def keys_kernel(lat_ref, gain_ref, wk_ref, wv_ref, kv_ref, normed_ref):
    x = lat_ref[...].astype(f32)
    normed_ref[...] = (x * inverse_rms(x) * gain_ref[...]).astype(bf16)
    low = low_lanes(CAP)
    for quad in range(4):
        cols = slice(quad * 256, quad * 256 + 256)
        k = dot(normed_ref[...], wk_ref[:, cols])
        v = dot(normed_ref[...], wv_ref[:, cols])
        for half in range(2):
            head = quad * 4 + half * 2
            part = slice(half * 128, half * 128 + 128)
            kp, vp = k[:, part], v[:, part]
            kv_ref[head] = jnp.where(low, kp, swap(vp)).astype(bf16)
            kv_ref[head + 1] = jnp.where(low, swap(kp), vp).astype(bf16)


def fold_heads(x, refs):
    for i, ref in enumerate(refs):
        for pair in range(HEADS // 2):
            part = x[i * HALF : (i + 1) * HALF, pair * 128 : pair * 128 + 128]
            first, second = fold(part[:64], part[64:])
            ref[2 * pair, 0:64, :] = first.astype(bf16)
            ref[2 * pair + 1, 0:64, :] = second.astype(bf16)


def unfold_heads(refs, rows_ref):
    for i, ref in enumerate(refs):
        for pair in range(HEADS // 2):
            first, second = fold(ref[2 * pair, 0:64, :].astype(f32), ref[2 * pair + 1, 0:64, :].astype(f32))
            cols = slice(pair * 128, pair * 128 + 128)
            rows_ref[i * HALF : i * HALF + 64, cols] = first.astype(bf16)
            rows_ref[i * HALF + 64 : (i + 1) * HALF, cols] = second.astype(bf16)


def parts(ref, n):
    return [ref.at[:, i * 64 : i * 64 + 64, :] for i in range(n)]


def queries_kernel(normed_ref, wq_ref, *q_refs):
    q = dot(normed_ref[...], wq_ref[...]) * 0.125
    fold_heads(q, [part for ref in q_refs for part in parts(ref, 2 // len(q_refs))])


def compact_kernel(counts_ref, kv_ref, kvx_ref, kvt_ref, rows_ref):
    sub = lax.broadcasted_iota(jnp.int32, (1, 8, 128), 1)
    row = lax.broadcasted_iota(jnp.int32, (CAP, 128), 0)
    rows_ref[...] = jnp.zeros((COLS, 128), f32)

    def place(b, off):
        count = counts_ref[b]
        shift = off & 7
        base = pl.multiple_of(off - shift + R, 8)
        x = jnp.where(row < count, kv_ref[b].astype(f32), 0.0)
        turned = pltpu.roll(x.reshape(32, 8, 128), shift, axis=1)
        before = rows_ref[pl.ds(base, 8), :].reshape(1, 8, 128)
        shifted = jnp.concatenate([before, turned], 0)
        turned = jnp.concatenate([turned, jnp.zeros((1, 8, 128), f32)], 0)
        rows_ref[pl.ds(base, 264), :] = jnp.where(sub < shift, shifted, turned).reshape(264, 128)
        return off + count

    total = lax.fori_loop(0, BANDS, place, jnp.int32(0))
    kvt_ref[128:, :] = jnp.ones((TURNED - 128, COLS), bf16)
    lane = lanes(128)
    tile_row = lax.broadcasted_iota(jnp.int32, (128, 128), 0)
    ones = jnp.where(lane < BIAS - ONES, 1.0, 0.0)
    for t in range(COLS // 128):
        span = slice(t * 128, t * 128 + 128)
        position = tile_row + (t * 128 - R)
        side = jnp.where((lane == BIAS - ONES) & ((position < 0) | (position >= total)), DEAD, ones)
        if R <= t * 128 < R + BANDS * CAP:
            tile = rows_ref[span, :]
            kvx_ref[span, :128] = tile.astype(bf16)
            kvx_ref[span, 128:] = jnp.where(lane < HEAD, side, swap(tile)).astype(bf16)
            kvt_ref[:128, span] = tile.T.astype(bf16)
        else:
            kvx_ref[span, :128] = jnp.zeros((128, 128), bf16)
            kvx_ref[span, 128:] = side.astype(bf16)
            kvt_ref[:128, span] = jnp.zeros((128, 128), bf16)


def query_columns(q, log_sum):
    lane = lanes(CAP)
    low = lane < HEAD
    scaled = q * LOG2E
    high = scaled.astype(bf16).astype(f32)
    rest = jnp.where(low, scaled - high, 0.0)
    second = jnp.where(low, 0.0, swap(rest))
    second = jnp.where(lane == BIAS - ONES, 1.0, second)
    if log_sum is not None:
        for i, piece in enumerate(split3(-log_sum)):
            second = jnp.where(lane == i, piece, second)
    return jnp.concatenate([jnp.where(low, high, 0.0), second], 1).astype(bf16)


def masked(p, first, size, rel):
    gap = lax.broadcasted_iota(jnp.int32, (EDGE, CAP), 0) - lax.broadcasted_iota(
        jnp.int32, (EDGE, CAP), 1
    )
    if first == 0:
        edge = jnp.where(gap >= rel, p[:EDGE], 0.0)
        p = edge if size == EDGE else jnp.concatenate([edge, p[EDGE:]], 0)
    if first + size == WIDTH:
        edge = jnp.where(gap <= rel, p[size - EDGE :], 0.0)
        p = edge if size == EDGE else jnp.concatenate([p[: size - EDGE], edge], 0)
    return p


def each_band(counts_ref, band):
    def some(i, off):
        for j in range(UNROLL):
            b = UNROLL * i + j
            band(b, pl.multiple_of(off - (off & 127), 128), off & 127)
            off = off + counts_ref[b]
        return off

    lax.fori_loop(0, BANDS // UNROLL, some, jnp.int32(0))


def forward_kernel(counts_ref, kvx_ref, kvt_ref, q_ref, mixed_ref, exact_ref):
    low = low_lanes(CAP)

    def band(b, start, rel):
        q = query_columns(unfold(q_ref[b]), None)
        out = jnp.zeros((TURNED - HEAD, CAP), f32)
        for first, size in STEPS:
            span = pl.ds(pl.multiple_of(start + first, 128), size)
            p = masked(jnp.exp2(dot_nt(kvx_ref[span, :], q)), first, size, rel)
            out = out + dot(kvt_ref[HEAD:, span], p.astype(bf16))
        out = jnp.concatenate([out, jnp.zeros((128 + HEAD - TURNED, CAP), f32)], 0).T
        total = jnp.broadcast_to(out[:, HEAD : HEAD + 1], (CAP, 128))
        out = jnp.where(low, out * (1.0 / total), jnp.log2(total))
        exact_ref[b] = out
        mixed_ref[b] = refold(out).astype(bf16)

    each_band(counts_ref, band)


def head_kernel(halves, mixed_ref, lat_ref, wo_ref, gain_ref, wh_ref, hidden_ref, pred_ref, rows_ref):
    unfold_heads(parts(mixed_ref, len(halves)), rows_ref)
    hidden = lat_ref[...].astype(f32) + dot(rows_ref[...], wo_ref[...])
    hidden_ref[...] = hidden
    head_in = (hidden * inverse_rms(hidden) * gain_ref[...]).astype(bf16)
    predicted = dot(head_in, wh_ref[...]).astype(bf16)
    for j in range(MEMBERS):
        pred_ref[j] = predicted


def loss_kernel(
    halves, last, place_ref, counts_ref, pred_ref, obs_ref, area_ref, hidden_ref, gain_ref, wh_ref, wo_ref,
    *refs,
):
    refs = list(refs)
    before = None if halves[0] == 0 else (refs.pop(0), refs.pop(0))
    grad_ref, out_ref = refs[:2]
    me, band = place_ref[0], place_ref[1]
    total = lax.fori_loop(0, BANDS, lambda b, t: t + counts_ref[b], jnp.int32(0))
    area = area_ref[...]
    rows = HALF * len(halves)
    weight = jnp.concatenate(
        [jnp.broadcast_to(area[i : i + 1, :], (128, 128)).T for i in halves], 0
    )
    row = lax.broadcasted_iota(jnp.int32, (rows, CH), 0) + halves[0] * HALF
    weight = jnp.where(row < counts_ref[band], weight, 0.0) / (total.astype(f32) * CH)
    mine = pred_ref[me].astype(f32)

    def smooth(gap):
        square = gap * gap + SMOOTH
        inverse = lax.rsqrt(square)
        return square * inverse, gap * inverse

    size, slope = smooth(mine - obs_ref[...].astype(f32))
    pair_size = jnp.zeros((rows, CH), f32)
    pair_slope = jnp.zeros((rows, CH), f32)
    for k in range(MEMBERS):
        a, da = smooth(mine - pred_ref[k].astype(f32))
        pair_size = pair_size + jnp.where(me == k, 0.0, 1.0) * a
        pair_slope = pair_slope + da
    loss = jnp.sum(weight * (size / MEMBERS - (0.5 * PAIR_SCALE) * pair_size), axis=0, keepdims=True)
    grad_pred = (weight * (slope / MEMBERS - PAIR_SCALE * pair_slope)).astype(bf16)

    hidden = hidden_ref[...]
    gain = gain_ref[...]
    inverse = inverse_rms(hidden)
    scaled = dot_nt(grad_pred, wh_ref[...]) * gain
    grad_hidden = norm_backward(hidden, inverse, scaled)
    grad_ref[...] = grad_hidden
    fold_heads(dot_nt(grad_hidden.astype(bf16), wo_ref[...]), parts(out_ref, len(halves)))

    head_in = (hidden * inverse * gain).astype(bf16)
    grad_head = dot_tn(head_in, grad_pred)
    if before is not None:
        grad_head = grad_head + before[0][...]
        loss = loss + before[1][0:1, :]
    if not last:
        refs[2][...] = grad_head
        refs[3][...] = jnp.broadcast_to(loss, (8, 128))
        return
    pieces = jnp.concatenate(list(split3(loss)) + [jnp.zeros((13, 128), f32)], 0).astype(bf16)
    sent_ref = refs[2]
    for b in range(BANDS):
        sent_ref[b, :HEAD_ROWS, :] = grad_head[b * HEAD_ROWS : (b + 1) * HEAD_ROWS].astype(bf16)
        sent_ref[b, HEAD_ROWS:, :] = pieces


def share_kernel(sent_ref, out_ref):
    grad = jnp.zeros((HEAD_ROWS, CH), f32)
    loss = jnp.zeros((16, 128), f32)
    for b in range(BANDS):
        grad = grad + sent_ref[b, :HEAD_ROWS, :].astype(f32)
        loss = loss + sent_ref[b, HEAD_ROWS:, :].astype(f32)
    loss = jnp.sum(loss, axis=0, keepdims=True)
    pieces = jnp.concatenate(list(split3(loss)) + [jnp.zeros((13, 128), f32)], 0).astype(bf16)
    grad = grad.astype(bf16)
    for j in range(MEMBERS):
        out_ref[j, :HEAD_ROWS, :] = grad
        out_ref[j, HEAD_ROWS:, :] = pieces


def total_kernel(shared_ref, grad_ref, loss_ref):
    grad = jnp.zeros((HEAD_ROWS, CH), f32)
    loss = jnp.zeros((16, 128), f32)
    for j in range(MEMBERS):
        grad = grad + shared_ref[j, :HEAD_ROWS, :].astype(f32)
        loss = loss + shared_ref[j, HEAD_ROWS:, :].astype(f32)
    grad_ref[...] = grad
    loss_ref[...] = jnp.sum(jnp.sum(loss, axis=0, keepdims=True), axis=1, keepdims=True)


def backward_kernel(counts_ref, kvx_ref, kvt_ref, q_ref, g_ref, exact_ref, dq_ref, acc_ref):
    acc_ref[...] = jnp.zeros((128, COLS), f32)
    low, lane = low_lanes(CAP), lanes(CAP)

    def band(b, start, rel):
        q = unfold(q_ref[b])
        g = unfold(g_ref[b])
        exact = exact_ref[b]
        inner = jnp.broadcast_to(
            jnp.sum(jnp.where(low, g * exact, 0.0), axis=1, keepdims=True), (CAP, 128)
        )
        right = query_columns(q, swap(exact))
        both = jnp.where(low, q, swap(g)).T.astype(bf16)
        side = jnp.zeros((CAP, 128), f32)
        for j, piece in enumerate(split3(-inner)):
            side = jnp.where(lane == j, piece, side)
        up = jnp.concatenate([jnp.where(low, 0.0, swap(g)), side], 1).astype(bf16)
        dq = jnp.zeros((HEAD, CAP), f32)
        for first, size in STEPS:
            span = pl.ds(pl.multiple_of(start + first, 128), size)
            kvx = kvx_ref[span, :]
            p = masked(jnp.exp2(dot_nt(kvx, right)), first, size, rel)
            ds = (p * dot_nt(kvx, up)).astype(bf16)
            acc_ref[:HEAD, span] += dot_nt(both[:HEAD], ds)
            acc_ref[HEAD:, span] += dot_nt(both[HEAD:], p.astype(bf16))
            dq = dq + dot(kvt_ref[:HEAD, span], ds)
        dq = jnp.concatenate([dq * 0.125, jnp.zeros((HEAD, CAP), f32)], 0).T
        dq_ref[b] = refold(dq).astype(bf16)

    each_band(counts_ref, band)


def give_kernel(counts_ref, acc_ref, out_ref, rows_ref):
    for t in range(R // 128, (R + BANDS * CAP) // 128 + 1):
        rows_ref[t * 128 : t * 128 + 128, :] = acc_ref[:, t * 128 : t * 128 + 128].T
    sub = lax.broadcasted_iota(jnp.int32, (1, 8, 128), 1)
    row = lax.broadcasted_iota(jnp.int32, (CAP, 128), 0)

    def give(b, off):
        count = counts_ref[b]
        shift = off & 7
        base = pl.multiple_of(off - shift + R, 8)
        x = rows_ref[pl.ds(base, 264), :].reshape(33, 8, 128)
        turned = pltpu.roll(x, (8 - shift) & 7, axis=1)
        x = jnp.where(sub + shift < 8, turned[:32], turned[1:]).reshape(CAP, 128)
        out_ref[b] = jnp.where(row < count, x, 0.0).astype(bf16)
        return off + count

    lax.fori_loop(0, BANDS, give, jnp.int32(0))


def grad_q_kernel(*refs):
    *dq_refs, wq_ref, out_ref, rows_ref = refs
    unfold_heads([part for ref in dq_refs for part in parts(ref, 2 // len(dq_refs))], rows_ref)
    out_ref[...] = dot_nt(rows_ref[...], wq_ref[...])


def latent_kernel(*refs):
    d_ref, part_ref, lat_ref, gain_ref, wk_ref, wv_ref, *grad_refs, out_ref, dk_ref, dv_ref = refs
    low = low_lanes(CAP)
    for pair in range(HEADS // 2):
        cols = slice(pair * 128, pair * 128 + 128)
        first = d_ref[2 * pair].astype(f32)
        second = d_ref[2 * pair + 1].astype(f32)
        dk_ref[:, cols] = jnp.where(low, first, swap(second)).astype(bf16)
        dv_ref[:, cols] = jnp.where(low, swap(first), second).astype(bf16)
    normed = (
        part_ref[...] + dot_nt(dk_ref[...], wk_ref[...]) + dot_nt(dv_ref[...], wv_ref[...])
    )
    x = lat_ref[...].astype(f32)
    out = norm_backward(x, inverse_rms(x), normed * gain_ref[...])
    rows = CAP // len(grad_refs)
    for i, ref in enumerate(grad_refs):
        part = slice(i * rows, i * rows + rows)
        out_ref[part, :] = (ref[...] + out[part]).astype(bf16)


VMEM_MIB = dict(
    keys=12, queries=8, compact=16, forward=16, head=12, loss=20, share=4, total=2, backward=24,
    give=12, grad_q=10, latent=20,
)


def call(name, kernel, outs, scalars, arrays, scratch=()):
    vmem = pl.BlockSpec(memory_space=pltpu.VMEM)
    smem = pl.BlockSpec(memory_space=pltpu.SMEM)
    return pl.pallas_call(
        kernel,
        out_shape=tuple(jax.ShapeDtypeStruct(s, d) for s, d in outs),
        in_specs=[smem] * len(scalars) + [vmem] * len(arrays),
        out_specs=tuple(vmem for _ in outs),
        scratch_shapes=[pltpu.VMEM(s, d) for s, d in scratch],
        compiler_params=pltpu.CompilerParams(vmem_limit_bytes=VMEM_MIB[name] << 20),
        name=name,
    )(*scalars, *arrays)


def exchange(x, axis):
    return lax.all_to_all(x, axis, split_axis=0, concat_axis=0, tiled=True)


STREAMS = ((0, 1),)


def body(
    latent, observed, area_weight, counts, gain_attn, w_query, w_key, w_value, w_out, gain_head, w_head
):
    members, cap, width = latent.shape
    lat = latent.reshape(cap, width)
    gain_a = gain_attn.reshape(1, width)
    gain_h = gain_head.reshape(1, width)
    area = area_weight.reshape(2, 128)
    place = jnp.stack([lax.axis_index("member"), lax.axis_index("band")]).astype(jnp.int32)

    def rows(x, halves):
        return x[halves[0] * HALF : (halves[-1] + 1) * HALF]

    kv, normed = call(
        "keys", keys_kernel, [((HEADS, cap, 128), bf16), ((cap, width), bf16)], [], [lat, gain_a, w_key, w_value]
    )
    kv = exchange(kv, "band")
    packed = [((HEADS, 64 * len(halves), 128), bf16) for halves in STREAMS]
    qs = call("queries", queries_kernel, packed, [], [normed, w_query])
    qs = [exchange(q, "band") for q in qs]
    keys = call(
        "compact",
        compact_kernel,
        [((COLS, DEPTH), bf16), ((TURNED, COLS), bf16)],
        [counts],
        [kv],
        [((COLS, 128), f32)],
    )
    mixed, exact = [], []
    for i, halves in enumerate(STREAMS):
        m, e = call(
            "forward",
            forward_kernel,
            [packed[i], ((BANDS, CAP, 128), f32)],
            [counts],
            [*keys, qs[i]],
        )
        mixed.append(exchange(m, "band"))
        exact.append(e)
    hidden, predicted = [], []
    for i, halves in enumerate(STREAMS):
        h, p = call(
            "head",
            functools.partial(head_kernel, halves),
            [((HALF * len(halves), width), f32), ((MEMBERS, HALF * len(halves), CH), bf16)],
            [],
            [mixed[i], rows(lat, halves), w_out, gain_h, w_head],
            [((HALF * len(halves), width), bf16)],
        )
        hidden.append(h)
        predicted.append(exchange(p, "member"))
    grad_hidden, gs, before = [], [], []
    for i, halves in enumerate(STREAMS):
        last = i == len(STREAMS) - 1
        extra = (
            [((BANDS, HEAD_ROWS + 16, 128), bf16)] if last else [((width, CH), f32), ((8, 128), f32)]
        )
        gh, g, *before = call(
            "loss",
            functools.partial(loss_kernel, halves, last),
            [((HALF * len(halves), width), f32), packed[i]] + extra,
            [place, counts],
            [predicted[i], rows(observed, halves), area, hidden[i], gain_h, w_head, w_out] + before,
        )
        grad_hidden.append(gh)
        gs.append(exchange(g, "band"))
    sent = exchange(before[0], "band")
    dqs, acc = [], []
    for i, halves in enumerate(STREAMS):
        dq, *acc = call(
            "backward",
            backward_kernel,
            [packed[i], ((128, COLS), f32)],
            [counts],
            [*keys, qs[i], gs[i], exact[i]],
        )
        dqs.append(exchange(dq, "band"))
    (shared,) = call("share", share_kernel, [((MEMBERS, HEAD_ROWS + 16, 128), bf16)], [], [sent])
    shared = exchange(shared, "member")
    (dkv,) = call(
        "give", give_kernel, [((BANDS, cap, 128), bf16)], [counts], acc, [((COLS, 128), f32)]
    )
    dkv = exchange(dkv, "band")
    (part,) = call(
        "grad_q", grad_q_kernel, [((cap, width), f32)], [], dqs + [w_query], [((cap, width), bf16)]
    )
    grad_head, loss = call(
        "total", total_kernel, [((HEAD_ROWS, CH), f32), ((1, 1), f32)], [], [shared]
    )
    (grad_latent,) = call(
        "latent",
        latent_kernel,
        [((cap, width), bf16)],
        [],
        [dkv, part, lat, gain_a, w_key, w_value] + grad_hidden,
        [((cap, width), bf16)] * 2,
    )
    return grad_latent.reshape(latent.shape), grad_head, loss.reshape(())


def solution(mesh):
    rows = P("member", "band", None)
    placed = (rows, P("band", None), P("band")) + (P(),) * 8
    return jax.shard_map(
        body,
        mesh=mesh,
        in_specs=placed,
        out_specs=(rows, P("band", None), P()),
        check_vma=False,
    )
```

```python
import jax
import jax.numpy as jnp
from jax import lax
from jax.experimental import pallas as pl
from jax.experimental.pallas import tpu as pltpu
from jax.sharding import PartitionSpec as P


HEADS = 16
HEAD = 64
CH = 128
R = 512
CAP = 256
MEMBERS = 8
BANDS = 16
LOG2E = 1.4426950408889634
EPS = 1e-06
SMOOTH = 0.0625
FAIR = 1.0 - 0.05 / MEMBERS
PAIR_SCALE = FAIR / (MEMBERS * (MEMBERS - 1.0))

HALF = CAP // 2
WIDTH = 2 * R + CAP + 128
ROWS = BANDS * CAP - CAP + WIDTH
EDGE = CAP + 128
CHUNKS = ((0, 512), (512, 512), (1024, 384))
TURNED = 144
DEAD = -32768.0
HEAD_ROWS = 64

f32 = jnp.float32
bf16 = jnp.bfloat16


def dot(a, b):
    return lax.dot_general(a, b, (((1,), (0,)), ((), ())), preferred_element_type=f32)


def dot_tn(a, b):
    return lax.dot_general(a, b, (((0,), (0,)), ((), ())), preferred_element_type=f32)


def swap(x):
    return pltpu.roll(x, HEAD, axis=1)


def low_lanes(rows):
    return lax.broadcasted_iota(jnp.int32, (rows, 128), 1) < HEAD


def fold(first, second):
    low = low_lanes(64)
    return jnp.where(low, first, swap(second)), jnp.where(low, swap(first), second)


def unfold(packed):
    packed = packed.astype(f32)
    other = swap(packed)
    return jnp.concatenate([packed[:64], other[:64], packed[64:], other[64:]], 0)


def refold(rows):
    return jnp.concatenate(
        [jnp.concatenate([rows[i : i + 64], rows[i + 64 : i + 128]], 1) for i in (0, 128)], 0
    )


def split3(x):
    high = x.astype(bf16).astype(f32)
    middle = (x - high).astype(bf16).astype(f32)
    return high, middle, (x - high - middle).astype(bf16).astype(f32)


def inverse_rms(x):
    return lax.rsqrt(jnp.mean(x * x, axis=-1, keepdims=True) + EPS)


def norm_backward(x, inverse, scaled):
    return inverse * scaled - x * (inverse * inverse * inverse) * jnp.mean(
        x * scaled, axis=-1, keepdims=True
    )


def fetch(copies, sems):
    started = [pltpu.make_async_copy(a, b, sems.at[i]) for i, (a, b) in enumerate(copies)]
    for copy in started:
        copy.start()

    def wait(count):
        for _ in range(count):
            started.pop(0).wait()

    return wait


def project_kernel(
    gain_ref, lat_hbm, wq_hbm, wk_hbm, wv_hbm, out_ref, lat_ref, wq_ref, wk_ref, wv_ref, sems
):
    wait = fetch([(lat_hbm, lat_ref), (wk_hbm, wk_ref), (wv_hbm, wv_ref), (wq_hbm, wq_ref)], sems)
    wait(1)
    x = lat_ref[...].astype(f32)
    normed = (x * inverse_rms(x) * gain_ref[...]).astype(bf16)
    low = low_lanes(CAP)
    wait(2)
    for quad in range(4):
        cols = slice(quad * 256, quad * 256 + 256)
        k = dot(normed, wk_ref[:, cols])
        v = dot(normed, wv_ref[:, cols])
        for half in range(2):
            head = quad * 4 + half * 2
            part = slice(half * 128, half * 128 + 128)
            kp, vp = k[:, part], v[:, part]
            out_ref[head, 128:, :] = jnp.where(low, kp, swap(vp)).astype(bf16)
            out_ref[head + 1, 128:, :] = jnp.where(low, swap(kp), vp).astype(bf16)
    wait(1)
    fold_heads(dot(normed, wq_ref[...]) * 0.125, parts(out_ref, 2))


def fold_heads(x, refs):
    for i, ref in enumerate(refs):
        for pair in range(HEADS // 2):
            part = x[i * HALF : (i + 1) * HALF, pair * 128 : pair * 128 + 128]
            first, second = fold(part[:64], part[64:])
            ref[2 * pair, 0:64, :] = first.astype(bf16)
            ref[2 * pair + 1, 0:64, :] = second.astype(bf16)


def unfold_heads(refs, rows_ref):
    for i, ref in enumerate(refs):
        for pair in range(HEADS // 2):
            first, second = fold(ref[2 * pair, 0:64, :].astype(f32), ref[2 * pair + 1, 0:64, :].astype(f32))
            cols = slice(pair * 128, pair * 128 + 128)
            rows_ref[i * HALF : i * HALF + 64, cols] = first.astype(bf16)
            rows_ref[i * HALF + 64 : (i + 1) * HALF, cols] = second.astype(bf16)


def parts(ref, n):
    return [ref.at[:, i * 64 : i * 64 + 64, :] for i in range(n)]


def turn_kernel(*refs):
    n = (len(refs) - 2) // 3
    w_hbm, outs, w_refs = refs[:n], refs[n : 2 * n], refs[2 * n : 3 * n]
    turned_ref, sems = refs[3 * n :]
    wait = fetch(list(zip(w_hbm, w_refs)), sems)
    for k, (w_ref, out) in enumerate(zip(w_refs, outs)):
        wait(1)
        rows = w_ref.shape[0]
        to = out if k < 2 else turned_ref
        for i in range(0, rows, 128):
            to[:, i : i + 128] = w_ref[i : i + 128, :].astype(f32).T.astype(bf16)
        if k >= 2:
            fetch([(turned_ref, out)], sems)(1)


def offsets(counts_ref, off_ref):
    def step(b, off):
        off_ref[b] = off
        return off + counts_ref[b]

    total = lax.fori_loop(0, BANDS, step, jnp.int32(0))
    off_ref[BANDS] = total
    return total


def compact(counts_ref, off_ref, x_ref, total, kv_ref, side_ref, kvt_ref, rows_ref):
    sub = lax.broadcasted_iota(jnp.int32, (1, 8, 128), 1)
    row = lax.broadcasted_iota(jnp.int32, (CAP, 128), 0)
    rows_ref[...] = jnp.zeros((ROWS, 128), f32)

    def place(b, carry):
        off = off_ref[b]
        shift = off & 7
        base = pl.multiple_of(off - shift + R, 8)
        x = jnp.where(row < counts_ref[b], x_ref[b, 128:, :].astype(f32), 0.0)
        turned = pltpu.roll(x.reshape(32, 8, 128), shift, axis=1)
        before = rows_ref[pl.ds(base, 8), :].reshape(1, 8, 128)
        shifted = jnp.concatenate([before, turned], 0)
        turned = jnp.concatenate([turned, jnp.zeros((1, 8, 128), f32)], 0)
        rows_ref[pl.ds(base, 264), :] = jnp.where(sub < shift, shifted, turned).reshape(264, 128)
        return carry

    lax.fori_loop(0, BANDS, place, 0)
    kvt_ref[128:, :] = jnp.ones((TURNED - 128, ROWS), bf16)
    lane = lax.broadcasted_iota(jnp.int32, (128, 128), 1)
    none = jnp.where(lane == 0, DEAD, 0.0)
    tile_row = lax.broadcasted_iota(jnp.int32, (128, 128), 0)
    for t in range(ROWS // 128):
        span = slice(t * 128, t * 128 + 128)
        bias = none if t * 128 < R else jnp.where(tile_row >= total + (R - t * 128), none, 0.0)
        if R <= t * 128 < R + BANDS * CAP:
            tile = rows_ref[span, :]
            kv_ref[span, :] = tile.astype(bf16)
            side_ref[span, :] = jnp.where(lane < HEAD, bias, swap(tile)).astype(bf16)
            kvt_ref[:128, span] = tile.T.astype(bf16)
        else:
            kv_ref[span, :] = jnp.zeros((128, 128), bf16)
            side_ref[span, :] = bias.astype(bf16)
            kvt_ref[:128, span] = jnp.zeros((128, 128), bf16)


def window(off_ref, k):
    off = off_ref[k]
    return pl.multiple_of(off - (off & 127), 128), off & 127


def masked(e, first, least):
    gap = lax.broadcasted_iota(jnp.int32, (EDGE, CAP), 0) - lax.broadcasted_iota(
        jnp.int32, (EDGE, CAP), 1
    )
    if first == 0:
        return jnp.concatenate([jnp.where(gap >= least, e[:EDGE], 0.0), e[EDGE:]], 0)
    return e if first < 2 * R else jnp.where(gap <= least, e, 0.0)


def by_two(count, step):
    def two(i, carry):
        for j in range(2):
            step(2 * i + j, j)
        return carry

    lax.fori_loop(0, count // 2, two, 0)


def forward_kernel(counts_ref, x_ref, *refs):
    blocks = BANDS
    mixed_ref, inverse_ref, e_hbm, kv_hbm, kt_hbm, q_hbm, own_hbm = refs[:7]
    off_ref, kv_ref, side_ref, kvt_ref, rows_ref = refs[7:12]
    qx0, qx1, e0, e1, out0, out1, sems, e_sems = refs[-8:]
    qx, e_refs, outs = (qx0, qx1), (e0, e1), (out0, out1)
    q_ref = x_ref.at[:, pl.ds(0, 128), :]
    total = offsets(counts_ref, off_ref)
    compact(counts_ref, off_ref, x_ref, total, kv_ref, side_ref, kvt_ref, rows_ref)
    give = fetch([(kv_ref, kv_hbm), (kvt_ref.at[pl.ds(0, HEAD), :], kt_hbm), (q_ref, q_hbm)], sems)
    lane = lax.broadcasted_iota(jnp.int32, (CAP, 128), 1)
    low = lane < HEAD
    one = jnp.where(lane == 0, 1.0, 0.0)

    def prepare(k, slot):
        scaled = jnp.where(low, unfold(q_ref[k]), 0.0) * LOG2E
        high = scaled.astype(bf16).astype(f32)
        columns = jnp.concatenate([high, jnp.where(low, one, swap(scaled - high))], 1)
        qx[slot][...] = columns.T.astype(bf16)

    def copy(k, slot):
        return pltpu.make_async_copy(e_refs[slot], e_hbm.at[k], e_sems.at[slot])

    def finish(k, slot):
        out = outs[slot][...]
        inverse = 1.0 / out[HEAD : HEAD + 1, :]
        inverse_ref[pl.ds(k, 1), :] = inverse
        mixed_ref[k] = refold((out[:HEAD] * inverse).T).astype(bf16)

    prepare(0, 0)

    def step(k, j):
        other = 1 - j

        @pl.when(k > 1)
        def _():
            copy(k - 2, j).wait()

        start, least = window(off_ref, k)
        out = None
        for first, size in CHUNKS:
            span = pl.ds(pl.multiple_of(start + first, 128), size)
            rows = jnp.concatenate([kv_ref[span, :], side_ref[span, :]], 1)
            e = masked(jnp.exp2(dot(rows, qx[j][...])), first, least)
            e_refs[j][first : first + size, :] = e.astype(bf16)
            part = dot(kvt_ref[HEAD:, span], e_refs[j][first : first + size, :])
            out = part if out is None else out + part
        outs[j][...] = out
        finish(jnp.maximum(k - 1, 0), other)
        prepare(jnp.minimum(k + 1, blocks - 1), other)
        copy(k, j).start()

    by_two(blocks, step)
    finish(blocks - 1, 1)
    give(3)
    fetch([(mixed_ref, own_hbm)], sems)(1)
    copy(blocks - 2, 0).wait()
    copy(blocks - 1, 1).wait()


def head_kernel(
    mixed_ref, wo_ref, gain_ref, wh_ref, lat_hbm, pred_ref, hidden_hbm, rows_ref, lat_ref, hidden_ref, sems
):
    wait = fetch([(lat_hbm, lat_ref)], sems)
    unfold_heads(parts(mixed_ref, 2), rows_ref)
    hidden = dot(rows_ref[...], wo_ref[...])
    wait(1)
    hidden = hidden + lat_ref[...].astype(f32)
    hidden_ref[...] = hidden
    give = fetch([(hidden_ref, hidden_hbm)], sems)
    head_in = (hidden * inverse_rms(hidden) * gain_ref[...]).astype(bf16)
    predicted = dot(head_in, wh_ref[...]).astype(bf16)
    for j in range(MEMBERS):
        pred_ref[j] = predicted
    give(1)


def loss_kernel(
    counts_ref, pred_ref, area_ref, obs_ref, gain_ref, wh_ref, wo_ref, hidden_hbm,
    out_ref, sent_ref, grad_hbm, hidden_ref, grad_ref, sems,
):
    wait = fetch([(hidden_hbm, hidden_ref)], sems)
    me, band = lax.axis_index("member"), lax.axis_index("band")
    total = lax.fori_loop(0, BANDS, lambda b, t: t + counts_ref[b], jnp.int32(0))
    area = area_ref[...]
    weight = jnp.concatenate(
        [jnp.broadcast_to(area[i : i + 1, :], (128, 128)).T for i in range(2)], 0
    )
    row = lax.broadcasted_iota(jnp.int32, (CAP, CH), 0)
    weight = jnp.where(row < counts_ref[band], weight, 0.0) / (total.astype(f32) * CH)
    mine = pred_ref[me].astype(f32)

    def smooth(gap):
        square = gap * gap + SMOOTH
        inverse = lax.rsqrt(square)
        return square * inverse, gap * inverse

    size, slope = smooth(mine - obs_ref[...].astype(f32))
    pair_size = jnp.zeros((CAP, CH), f32)
    pair_slope = jnp.zeros((CAP, CH), f32)
    for k in range(MEMBERS):
        a, da = smooth(mine - pred_ref[k].astype(f32))
        pair_size = pair_size + jnp.where(me == k, 0.0, 1.0) * a
        pair_slope = pair_slope + da
    loss = jnp.sum(weight * (size / MEMBERS - (0.5 * PAIR_SCALE) * pair_size), axis=0, keepdims=True)
    grad_pred = (weight * (slope / MEMBERS - PAIR_SCALE * pair_slope)).astype(bf16)

    wait(1)
    hidden = hidden_ref[...]
    gain = gain_ref[...]
    inverse = inverse_rms(hidden)
    scaled = dot(grad_pred, wh_ref[...]) * gain
    grad_hidden = norm_backward(hidden, inverse, scaled)
    grad_ref[...] = grad_hidden
    give = fetch([(grad_ref, grad_hbm)], sems)
    fold_heads(dot(grad_hidden.astype(bf16), wo_ref[...]), parts(out_ref, 2))

    head_in = (hidden * inverse * gain).astype(bf16)
    grad_head = dot_tn(head_in, grad_pred)
    pieces = jnp.concatenate(list(split3(loss)) + [jnp.zeros((13, 128), f32)], 0).astype(bf16)
    for b in range(BANDS):
        sent_ref[b, :HEAD_ROWS, :] = grad_head[b * HEAD_ROWS : (b + 1) * HEAD_ROWS].astype(bf16)
        sent_ref[b, HEAD_ROWS:, :] = pieces
    give(1)


def share_kernel(sent_ref, out_ref):
    grad = jnp.zeros((HEAD_ROWS, CH), f32)
    loss = jnp.zeros((16, 128), f32)
    for b in range(BANDS):
        grad = grad + sent_ref[b, :HEAD_ROWS, :].astype(f32)
        loss = loss + sent_ref[b, HEAD_ROWS:, :].astype(f32)
    loss = jnp.sum(loss, axis=0, keepdims=True)
    pieces = jnp.concatenate(list(split3(loss)) + [jnp.zeros((13, 128), f32)], 0).astype(bf16)
    out_ref[:HEAD_ROWS, :] = grad.astype(bf16)
    out_ref[HEAD_ROWS:, :] = pieces


def total_kernel(me_ref, *refs):
    *shared_refs, grad_ref, loss_ref, all_ref = refs
    for k, ref in enumerate(shared_refs):
        all_ref[(me_ref[0] + MEMBERS - k) % MEMBERS] = ref[...]
    grad = jnp.zeros((HEAD_ROWS, CH), f32)
    loss = jnp.zeros((16, 128), f32)
    for j in range(MEMBERS):
        grad = grad + all_ref[j, :HEAD_ROWS, :].astype(f32)
        loss = loss + all_ref[j, HEAD_ROWS:, :].astype(f32)
    grad_ref[...] = grad
    loss_ref[...] = jnp.sum(jnp.sum(loss, axis=0, keepdims=True), axis=1, keepdims=True)


def backward_kernel(
    counts_ref, inverse_ref, q_hbm, g_hbm, mixed_hbm, kv_hbm, kt_hbm, p_hbm, out_hbm,
    off_ref, q_ref, g_ref, mixed_ref, kv_ref, kt_ref, acc_ref, dq_ref, dkv_ref,
    both0, both1, up0, up1, inner0, inner1, p0, p1, dq0, dq1, sems, p_sems, out_sems,
):
    blocks = BANDS
    boths, ups, inners, p_refs, dqs = (both0, both1), (up0, up1), (inner0, inner1), (p0, p1), (dq0, dq1)

    def copy(k, slot):
        return pltpu.make_async_copy(p_hbm.at[k], p_refs[slot], p_sems.at[slot])

    wait = fetch(
        [
            (q_hbm, q_ref),
            (g_hbm, g_ref),
            (mixed_hbm, mixed_ref),
            (kv_hbm, kv_ref),
            (kt_hbm, kt_ref),
        ],
        sems,
    )
    copy(0, 0).start()
    copy(1, 1).start()
    offsets(counts_ref, off_ref)
    acc_ref[...] = jnp.zeros((ROWS, 128), f32)
    low = low_lanes(CAP)

    def prepare(k, slot):
        q = unfold(q_ref[k])
        g = unfold(g_ref[k])
        mixed = unfold(mixed_ref[k])
        inner = jnp.sum(jnp.where(low, g * mixed, 0.0).T, axis=0, keepdims=True)
        inners[slot][...] = jnp.broadcast_to(inner, (8, CAP))
        boths[slot][:CAP, :] = jnp.where(low, q, 0.0).astype(bf16)
        g = jnp.where(low, 0.0, swap(g))
        boths[slot][CAP:, :] = g.astype(bf16)
        ups[slot][...] = g.T.astype(bf16)

    def finish(k, slot):
        dq_ref[k] = refold((dqs[slot][...] * 0.125).T).astype(bf16)

    wait(3)
    prepare(0, 0)
    wait(2)

    def step(k, j):
        other = 1 - j
        copy(k, j).wait()
        start, _ = window(off_ref, k)
        inner = inners[j][0:1, :]
        inverse = inverse_ref[pl.ds(k, 1), :]
        dq = None
        for first, size in CHUNKS:
            span = pl.ds(pl.multiple_of(start + first, 128), size)
            p = p_refs[j][first : first + size, :].astype(f32) * inverse
            ds = (p * (dot(kv_ref[span, :], ups[j][...]) - inner)).astype(bf16)
            acc_ref[span, :] += dot(jnp.concatenate([ds, p.astype(bf16)], 1), boths[j][...])
            part = dot(kt_ref[:, span], ds)
            dq = part if dq is None else dq + part
        dqs[j][...] = dq
        prepare(jnp.minimum(k + 1, blocks - 1), other)
        finish(jnp.maximum(k - 1, 0), other)

        @pl.when(k < blocks - 2)
        def _():
            copy(k + 2, j).start()

    by_two(blocks, step)
    finish(blocks - 1, 1)
    out_dq = pltpu.make_async_copy(dq_ref, out_hbm.at[:, pl.ds(0, 128), :], out_sems.at[0])
    out_dq.start()
    sub = lax.broadcasted_iota(jnp.int32, (1, 8, 128), 1)
    row = lax.broadcasted_iota(jnp.int32, (CAP, 128), 0)

    def give(b, carry):
        off = off_ref[b]
        shift = off & 7
        x = acc_ref[pl.ds(pl.multiple_of(off - shift + R, 8), 264), :].reshape(33, 8, 128)
        turned = pltpu.roll(x, (8 - shift) & 7, axis=1)
        x = jnp.where(sub + shift < 8, turned[:32], turned[1:]).reshape(CAP, 128)
        dkv_ref[b] = jnp.where(row < counts_ref[b], x, 0.0).astype(bf16)
        return carry

    some = BANDS // 4
    out_dkv = []
    for i in range(4):
        lax.fori_loop(i * some, (i + 1) * some, give, 0)
        bands = pl.ds(i * some, some)
        out_dkv.append(
            pltpu.make_async_copy(
                dkv_ref.at[bands], out_hbm.at[bands, pl.ds(128, CAP), :], out_sems.at[1 + i]
            )
        )
        out_dkv[-1].start()
    for out in [out_dq, *out_dkv]:
        out.wait()


def latent_kernel(
    d_ref, gain_ref, wq_hbm, wk_hbm, wv_hbm, lat_hbm, grad_hbm, out_ref,
    wq_ref, wk_ref, wv_ref, lat_ref, grad_ref, dq_ref, dk_ref, dv_ref, sems,
):
    wait = fetch(
        [(wq_hbm, wq_ref), (wk_hbm, wk_ref), (wv_hbm, wv_ref), (lat_hbm, lat_ref), (grad_hbm, grad_ref)],
        sems,
    )
    low = low_lanes(CAP)
    unfold_heads(parts(d_ref, 2), dq_ref)
    for pair in range(HEADS // 2):
        cols = slice(pair * 128, pair * 128 + 128)
        first = d_ref[2 * pair, 128:, :].astype(f32)
        second = d_ref[2 * pair + 1, 128:, :].astype(f32)
        dk_ref[:, cols] = jnp.where(low, first, swap(second)).astype(bf16)
        dv_ref[:, cols] = jnp.where(low, swap(first), second).astype(bf16)
    wait(1)
    normed = dot(dq_ref[...], wq_ref[...])
    wait(1)
    normed = normed + dot(dk_ref[...], wk_ref[...])
    wait(1)
    normed = normed + dot(dv_ref[...], wv_ref[...])
    wait(2)
    x = lat_ref[...].astype(f32)
    out = norm_backward(x, inverse_rms(x), normed * gain_ref[...])
    out_ref[...] = (grad_ref[...] + out).astype(bf16)


VMEM_MIB = dict(project=20, turn=20, forward=24, head=12, loss=20, share=8, total=8, latent=24)


def call(name, kernel, outs, scalars, arrays, held=(), held_out=(), scratch=(), sems=()):
    vmem = pl.BlockSpec(memory_space=pltpu.VMEM)
    smem = pl.BlockSpec(memory_space=pltpu.SMEM)
    hbm = pl.BlockSpec(memory_space=pltpu.HBM)
    return pl.pallas_call(
        kernel,
        out_shape=tuple(jax.ShapeDtypeStruct(s, d) for s, d in outs)
        + tuple(pltpu.HBM(s, d) for s, d in held_out),
        in_specs=[smem] * len(scalars) + [vmem] * len(arrays) + [hbm] * len(held),
        out_specs=(vmem,) * len(outs) + (hbm,) * len(held_out),
        scratch_shapes=[s if not isinstance(s, tuple) else pltpu.VMEM(*s) for s in scratch]
        + [pltpu.SemaphoreType.DMA((n,)) for n in sems],
        compiler_params=pltpu.CompilerParams(
            vmem_limit_bytes=VMEM_MIB[name] << 20 if name in VMEM_MIB else None
        ),
    )(*scalars, *arrays, *(pltpu.with_memory_space_constraint(a, pltpu.HBM) for a in held))


def exchange(x, axis):
    return lax.all_to_all(x, axis, split_axis=0, concat_axis=0, tiled=True)


def body(
    latent, observed, area_weight, counts, gain_attn, w_query, w_key, w_value, w_out, gain_head, w_head
):
    _, cap, width = latent.shape
    lat = latent.reshape(cap, width)
    gain_a = gain_attn.reshape(1, width)
    gain_h = gain_head.reshape(1, width)
    area = area_weight.reshape(2, 128)
    weight = ((width, width), bf16)
    offs = pltpu.SMEM((BANDS + 1,), jnp.int32)
    (x,) = call(
        "project",
        project_kernel,
        [((HEADS, 384, 128), bf16)],
        [],
        [gain_a],
        [lat, w_query, w_key, w_value],
        scratch=[((cap, width), bf16)] + [weight] * 3,
        sems=[4],
    )
    x, *weights = lax.optimization_barrier((x, w_head, w_out, w_query, w_key, w_value))
    turned = call(
        "turn",
        turn_kernel,
        [((CH, width), bf16), weight],
        [],
        [],
        weights,
        [weight] * 3,
        [((width, CH), bf16)] + [weight] * 5,
        [5],
    )
    x = exchange(x, "band")
    packed = ((BANDS, 128, 128), bf16)
    acc = ((ROWS, 128), f32)
    run = ((WIDTH, CAP), bf16)
    mixed, inverse, probs, kv, kt, q, own = call(
        "forward",
        forward_kernel,
        [packed, ((BANDS, CAP), f32)],
        [counts],
        [x],
        [],
        [((BANDS, WIDTH, CAP), bf16), ((ROWS, 128), bf16), ((HEAD, ROWS), bf16), packed, packed],
        [offs, ((ROWS, 128), bf16), ((ROWS, 128), bf16), ((TURNED, ROWS), bf16), acc]
        + [((256, CAP), bf16)] * 2
        + [run] * 2
        + [((TURNED - HEAD, CAP), f32)] * 2,
        [3, 2],
    )
    mixed = exchange(mixed, "band")
    predicted, hidden = call(
        "head",
        head_kernel,
        [((MEMBERS, cap, CH), bf16)],
        [],
        [mixed, w_out, gain_h, w_head],
        [lat],
        [((cap, width), f32)],
        [((cap, width), bf16)] * 2 + [((cap, width), f32)],
        sems=[1],
    )
    predicted = exchange(predicted, "member")
    g, sent, grad_hidden = call(
        "loss",
        loss_kernel,
        [packed, ((BANDS, HEAD_ROWS + 16, 128), bf16)],
        [counts],
        [predicted, area, observed, gain_h, turned[0], turned[1]],
        [hidden],
        [((cap, width), f32)],
        [((cap, width), f32)] * 2,
        [1],
    )
    g = exchange(g, "band")
    g, sent = lax.optimization_barrier((g, sent))
    sent = exchange(sent, "band")
    (d,) = call(
        "backward",
        backward_kernel,
        [],
        [counts],
        [inverse],
        [q, g, own, kv, kt, probs],
        [((BANDS, 384, 128), bf16)],
        [offs, packed, packed, packed, ((ROWS, 128), bf16), ((HEAD, ROWS), bf16), acc]
        + [packed, ((BANDS, CAP, 128), bf16)]
        + [((2 * CAP, 128), bf16)] * 2
        + [((128, CAP), bf16)] * 2
        + [((8, CAP), f32)] * 2
        + [run] * 2
        + [((HEAD, CAP), f32)] * 2,
        [5, 2, 5],
    )
    d, sent = lax.optimization_barrier((d, sent))
    d = exchange(d, "band")
    (share,) = call("share", share_kernel, [((HEAD_ROWS + 16, 128), bf16)], [], [sent])
    shared = [share]
    for k in range(1, MEMBERS):
        shared.append(lax.ppermute(share, "member", [(j, (j + k) % MEMBERS) for j in range(MEMBERS)]))
    me = lax.axis_index("member").astype(jnp.int32).reshape(1)
    grad_head, loss = call(
        "total",
        total_kernel,
        [((HEAD_ROWS, CH), f32), ((1, 1), f32)],
        [me],
        shared,
        scratch=[((MEMBERS, HEAD_ROWS + 16, 128), bf16)],
    )
    (grad_latent,) = call(
        "latent",
        latent_kernel,
        [((cap, width), bf16)],
        [],
        [d, gain_a],
        [turned[2], turned[3], turned[4], lat, grad_hidden],
        scratch=[weight] * 3
        + [((cap, width), bf16), ((cap, width), f32)]
        + [((cap, width), bf16)] * 3,
        sems=[5],
    )
    return grad_latent.reshape(latent.shape), grad_head, loss.reshape(())


def solution(mesh):
    rows = P("member", "band", None)
    placed = (rows, P("band", None), P("band")) + (P(),) * 8
    return jax.shard_map(
        body,
        mesh=mesh,
        in_specs=placed,
        out_specs=(rows, P("band", None), P()),
        check_vma=False,
    )
```

```python
import jax
import jax.numpy as jnp
from jax import lax
from jax.experimental import pallas as pl
from jax.experimental.pallas import tpu as pltpu
from jax.sharding import PartitionSpec as P


HEADS = 16
HEAD = 64
CH = 128
R = 512
CAP = 256
MEMBERS = 8
BANDS = 16
LOG2E = 1.4426950408889634
EPS = 1e-06
SMOOTH = 0.0625
FAIR = 1.0 - 0.05 / MEMBERS
PAIR_SCALE = FAIR / (MEMBERS * (MEMBERS - 1.0))

HALF = CAP // 2
WIDTH = 2 * R + CAP + 128
ROWS = BANDS * CAP - CAP + WIDTH
EDGE = CAP + 128
CHUNKS = ((0, 512), (512, 512), (1024, 384))
TURNED = 144
DEAD = -32768.0
UNROLL = 4
HEAD_ROWS = 64

f32 = jnp.float32
bf16 = jnp.bfloat16


def dot(a, b):
    return lax.dot_general(a, b, (((1,), (0,)), ((), ())), preferred_element_type=f32)


def dot_tn(a, b):
    return lax.dot_general(a, b, (((0,), (0,)), ((), ())), preferred_element_type=f32)


def swap(x):
    return pltpu.roll(x, HEAD, axis=1)


def low_lanes(rows):
    return lax.broadcasted_iota(jnp.int32, (rows, 128), 1) < HEAD


def fold(first, second):
    low = low_lanes(64)
    return jnp.where(low, first, swap(second)), jnp.where(low, swap(first), second)


def unfold(packed):
    packed = packed.astype(f32)
    other = swap(packed)
    return jnp.concatenate([packed[:64], other[:64], packed[64:], other[64:]], 0)


def refold(rows):
    return jnp.concatenate(
        [jnp.concatenate([rows[i : i + 64], rows[i + 64 : i + 128]], 1) for i in (0, 128)], 0
    )


def split3(x):
    high = x.astype(bf16).astype(f32)
    middle = (x - high).astype(bf16).astype(f32)
    return high, middle, (x - high - middle).astype(bf16).astype(f32)


def inverse_rms(x):
    return lax.rsqrt(jnp.mean(x * x, axis=-1, keepdims=True) + EPS)


def norm_backward(x, inverse, scaled):
    return inverse * scaled - x * (inverse * inverse * inverse) * jnp.mean(
        x * scaled, axis=-1, keepdims=True
    )


def fetch(copies, sems):
    started = [pltpu.make_async_copy(a, b, sems.at[i]) for i, (a, b) in enumerate(copies)]
    for copy in started:
        copy.start()

    def wait(count):
        for _ in range(count):
            started.pop(0).wait()

    return wait


def project_kernel(
    gain_hbm, lat_hbm, wq_hbm, wk_hbm, wv_hbm, out_ref, gain_ref, lat_ref, wq_ref, wk_ref, wv_ref, sems
):
    wait = fetch(
        [(gain_hbm, gain_ref), (lat_hbm, lat_ref), (wk_hbm, wk_ref), (wv_hbm, wv_ref), (wq_hbm, wq_ref)], sems
    )
    wait(2)
    x = lat_ref[...].astype(f32)
    normed = (x * inverse_rms(x) * gain_ref[...]).astype(bf16)
    low = low_lanes(CAP)
    wait(2)
    for quad in range(4):
        cols = slice(quad * 256, quad * 256 + 256)
        k = dot(normed, wk_ref[:, cols])
        v = dot(normed, wv_ref[:, cols])
        for half in range(2):
            head = quad * 4 + half * 2
            part = slice(half * 128, half * 128 + 128)
            kp, vp = k[:, part], v[:, part]
            out_ref[head, 128:, :] = jnp.where(low, kp, swap(vp)).astype(bf16)
            out_ref[head + 1, 128:, :] = jnp.where(low, swap(kp), vp).astype(bf16)
    wait(1)
    fold_heads(dot(normed, wq_ref[...]) * 0.125, parts(out_ref, 2))


def fold_heads(x, refs):
    for i, ref in enumerate(refs):
        for pair in range(HEADS // 2):
            part = x[i * HALF : (i + 1) * HALF, pair * 128 : pair * 128 + 128]
            first, second = fold(part[:64], part[64:])
            ref[2 * pair, 0:64, :] = first.astype(bf16)
            ref[2 * pair + 1, 0:64, :] = second.astype(bf16)


def unfold_heads(refs, rows_ref):
    for i, ref in enumerate(refs):
        for pair in range(HEADS // 2):
            first, second = fold(ref[2 * pair, 0:64, :].astype(f32), ref[2 * pair + 1, 0:64, :].astype(f32))
            cols = slice(pair * 128, pair * 128 + 128)
            rows_ref[i * HALF : i * HALF + 64, cols] = first.astype(bf16)
            rows_ref[i * HALF + 64 : (i + 1) * HALF, cols] = second.astype(bf16)


def parts(ref, n):
    return [ref.at[:, i * 64 : i * 64 + 64, :] for i in range(n)]


def turn_kernel(*refs):
    n = (len(refs) - 2) // 3
    w_hbm, outs, w_refs = refs[:n], refs[n : 2 * n], refs[2 * n : 3 * n]
    turned_ref, sems = refs[3 * n :]
    wait = fetch(list(zip(w_hbm, w_refs)), sems)
    for k, (w_ref, out) in enumerate(zip(w_refs, outs)):
        wait(1)
        rows = w_ref.shape[0]
        to = out if k < 2 else turned_ref
        for i in range(0, rows, 128):
            to[:, i : i + 128] = w_ref[i : i + 128, :].astype(f32).T.astype(bf16)
        if k >= 2:
            fetch([(turned_ref, out)], sems)(1)


def offsets(counts_ref, off_ref):
    def step(b, off):
        off_ref[b] = off
        return off + counts_ref[b]

    total = lax.fori_loop(0, BANDS, step, jnp.int32(0))
    off_ref[BANDS] = total
    return total


def compact(counts_ref, off_ref, x_ref, total, kv_ref, side_ref, kvt_ref, rows_ref):
    sub = lax.broadcasted_iota(jnp.int32, (1, 8, 128), 1)
    row = lax.broadcasted_iota(jnp.int32, (CAP, 128), 0)
    rows_ref[...] = jnp.zeros((ROWS, 128), f32)

    def place(b, carry):
        off = off_ref[b]
        shift = off & 7
        base = pl.multiple_of(off - shift + R, 8)
        x = jnp.where(row < counts_ref[b], x_ref[b, 128:, :].astype(f32), 0.0)
        turned = pltpu.roll(x.reshape(32, 8, 128), shift, axis=1)
        before = rows_ref[pl.ds(base, 8), :].reshape(1, 8, 128)
        shifted = jnp.concatenate([before, turned], 0)
        turned = jnp.concatenate([turned, jnp.zeros((1, 8, 128), f32)], 0)
        rows_ref[pl.ds(base, 264), :] = jnp.where(sub < shift, shifted, turned).reshape(264, 128)
        return carry

    lax.fori_loop(0, BANDS, place, 0)
    kvt_ref[128:, :] = jnp.ones((TURNED - 128, ROWS), bf16)
    lane = lax.broadcasted_iota(jnp.int32, (128, 128), 1)
    none = jnp.where(lane == 0, DEAD, 0.0)
    tile_row = lax.broadcasted_iota(jnp.int32, (128, 128), 0)
    for t in range(ROWS // 128):
        span = slice(t * 128, t * 128 + 128)
        bias = none if t * 128 < R else jnp.where(tile_row >= total + (R - t * 128), none, 0.0)
        if R <= t * 128 < R + BANDS * CAP:
            tile = rows_ref[span, :]
            kv_ref[span, :] = tile.astype(bf16)
            side_ref[span, :] = jnp.where(lane < HEAD, bias, swap(tile)).astype(bf16)
            kvt_ref[:128, span] = tile.astype(bf16).T
        else:
            kv_ref[span, :] = jnp.zeros((128, 128), bf16)
            side_ref[span, :] = bias.astype(bf16)
            kvt_ref[:128, span] = jnp.zeros((128, 128), bf16)


def window(off_ref, k):
    off = off_ref[k]
    return pl.multiple_of(off - (off & 127), 128), off & 127


def masked(e, first, least):
    gap = lax.broadcasted_iota(jnp.int32, (EDGE, CAP), 0) - lax.broadcasted_iota(
        jnp.int32, (EDGE, CAP), 1
    )
    if first == 0:
        return jnp.concatenate([jnp.where(gap >= least, e[:EDGE], 0.0), e[EDGE:]], 0)
    return e if first < 2 * R else jnp.where(gap <= least, e, 0.0)


def by_two(count, step):
    def some(i, carry):
        for j in range(UNROLL):
            step(UNROLL * i + j, j % 2)
        return carry

    lax.fori_loop(0, count // UNROLL, some, 0)


def forward_kernel(counts_ref, x_ref, *refs):
    blocks = BANDS
    mixed_ref, inverse_ref, e_hbm, kv_hbm, kt_hbm, q_hbm, own_hbm = refs[:7]
    off_ref, kv_ref, side_ref, kvt_ref, rows_ref = refs[7:12]
    qx0, qx1, e0, e1, out0, out1, sems, e_sems = refs[-8:]
    qx, e_refs, outs = (qx0, qx1), (e0, e1), (out0, out1)
    q_ref = x_ref.at[:, pl.ds(0, 128), :]
    total = offsets(counts_ref, off_ref)
    compact(counts_ref, off_ref, x_ref, total, kv_ref, side_ref, kvt_ref, rows_ref)
    give = fetch([(kv_ref, kv_hbm), (kvt_ref.at[pl.ds(0, HEAD), :], kt_hbm), (q_ref, q_hbm)], sems)
    lane = lax.broadcasted_iota(jnp.int32, (CAP, 128), 1)
    low = lane < HEAD
    one = jnp.where(lane == 0, 1.0, 0.0)

    def prepare(k, slot):
        scaled = jnp.where(low, unfold(q_ref[k]), 0.0) * LOG2E
        high = scaled.astype(bf16).astype(f32)
        columns = jnp.concatenate([high, jnp.where(low, one, swap(scaled - high))], 1)
        qx[slot][...] = columns.T.astype(bf16)

    def copy(k, slot):
        return pltpu.make_async_copy(e_refs[slot], e_hbm.at[k], e_sems.at[slot])

    def finish(k, slot):
        out = outs[slot][...]
        inverse = 1.0 / out[HEAD : HEAD + 1, :]
        inverse_ref[pl.ds(k, 1), :] = inverse
        mixed_ref[k] = refold((out[:HEAD] * inverse).T).astype(bf16)

    prepare(0, 0)

    def step(k, j):
        other = 1 - j

        @pl.when(k > 1)
        def _():
            copy(k - 2, j).wait()

        start, least = window(off_ref, k)
        out = None
        for first, size in CHUNKS:
            span = pl.ds(pl.multiple_of(start + first, 128), size)
            rows = jnp.concatenate([kv_ref[span, :], side_ref[span, :]], 1)
            e = masked(jnp.exp2(dot(rows, qx[j][...])), first, least)
            e_refs[j][first : first + size, :] = e.astype(bf16)
            part = dot(kvt_ref[HEAD:, span], e_refs[j][first : first + size, :])
            out = part if out is None else out + part
        outs[j][...] = out
        finish(jnp.maximum(k - 1, 0), other)
        prepare(jnp.minimum(k + 1, blocks - 1), other)
        copy(k, j).start()

    by_two(blocks, step)
    finish(blocks - 1, 1)
    give(3)
    fetch([(mixed_ref, own_hbm)], sems)(1)
    copy(blocks - 2, 0).wait()
    copy(blocks - 1, 1).wait()


def head_kernel(
    mixed_ref, wo_ref, gain_ref, wh_ref, lat_hbm, hidden_hbm, pred_hbm,
    rows_ref, lat_ref, hidden_ref, pred_ref, sems, hidden_sems, pred_sems,
):
    wait = fetch([(lat_hbm, lat_ref)], sems)
    unfold_heads(parts(mixed_ref, 2), rows_ref)
    wait(1)
    gives = []
    for i in range(4):
        cols = pl.ds(i * 256, 256)
        hidden_ref[:, cols] = lat_ref[:, cols].astype(f32) + dot(rows_ref[...], wo_ref[:, cols])
        gives.append(
            pltpu.make_async_copy(hidden_ref.at[:, cols], hidden_hbm.at[:, cols], hidden_sems.at[i])
        )
        gives[-1].start()
    hidden = hidden_ref[...]
    head_in = (hidden * inverse_rms(hidden) * gain_ref[...]).astype(bf16)
    pred_ref[...] = dot(head_in, wh_ref[...]).astype(bf16)
    out = fetch([(pred_ref, pred_hbm.at[j]) for j in range(MEMBERS)], pred_sems)
    for give in gives:
        give.wait()
    out(MEMBERS)


def loss_kernel(
    counts_ref, pred_ref, area_ref, obs_ref, gain_ref, wh_ref, wo_ref, hidden_hbm,
    grad_pred_ref, loss_ref, grad_hbm, out_hbm, hidden_ref, grad_ref, out_ref, sems, out_sems,
):
    wait = fetch([(hidden_hbm, hidden_ref)], sems)
    me, band = lax.axis_index("member"), lax.axis_index("band")
    total = lax.fori_loop(0, BANDS, lambda b, t: t + counts_ref[b], jnp.int32(0))
    area = area_ref[...]
    weight = jnp.concatenate(
        [jnp.broadcast_to(area[i : i + 1, :], (128, 128)).T for i in range(2)], 0
    )
    row = lax.broadcasted_iota(jnp.int32, (CAP, CH), 0)
    weight = jnp.where(row < counts_ref[band], weight, 0.0) / (total.astype(f32) * CH)
    mine = pred_ref[me].astype(f32)

    def smooth(gap):
        square = gap * gap + SMOOTH
        inverse = lax.rsqrt(square)
        return square * inverse, gap * inverse

    size, slope = smooth(mine - obs_ref[...].astype(f32))
    pair_size = jnp.zeros((CAP, CH), f32)
    pair_slope = jnp.zeros((CAP, CH), f32)
    for k in range(MEMBERS):
        a, da = smooth(mine - pred_ref[k].astype(f32))
        pair_size = pair_size + jnp.where(me == k, 0.0, 1.0) * a
        pair_slope = pair_slope + da
    loss = jnp.sum(weight * (size / MEMBERS - (0.5 * PAIR_SCALE) * pair_size), axis=0, keepdims=True)
    grad_pred = (weight * (slope / MEMBERS - PAIR_SCALE * pair_slope)).astype(bf16)

    wait(1)
    hidden = hidden_ref[...]
    gain = gain_ref[...]
    inverse = inverse_rms(hidden)
    scaled = dot(grad_pred, wh_ref[...]) * gain
    grad_hidden = norm_backward(hidden, inverse, scaled)
    grad_ref[...] = grad_hidden
    give = fetch([(grad_ref, grad_hbm)], sems)
    fold_heads(dot(grad_hidden.astype(bf16), wo_ref[...]), parts(out_ref, 2))
    out = fetch([(out_ref, out_hbm)], out_sems)
    grad_pred_ref[...] = grad_pred
    loss_ref[...] = jnp.broadcast_to(loss, (8, 128))
    give(1)
    out(1)


def grad_head_kernel(grad_pred_ref, loss_ref, gain_ref, hidden_hbm, sent_ref, hidden_ref, sems):
    fetch([(hidden_hbm, hidden_ref)], sems)(1)
    hidden = hidden_ref[...]
    head_in = (hidden * inverse_rms(hidden) * gain_ref[...]).astype(bf16)
    grad_head = dot_tn(head_in, grad_pred_ref[...])
    pieces = jnp.concatenate(
        list(split3(loss_ref[0:1, :])) + [jnp.zeros((13, 128), f32)], 0
    ).astype(bf16)
    for b in range(BANDS):
        sent_ref[b, :HEAD_ROWS, :] = grad_head[b * HEAD_ROWS : (b + 1) * HEAD_ROWS].astype(bf16)
        sent_ref[b, HEAD_ROWS:, :] = pieces


def share_kernel(sent_ref, out_ref):
    grad = jnp.zeros((HEAD_ROWS, CH), f32)
    loss = jnp.zeros((16, 128), f32)
    for b in range(BANDS):
        grad = grad + sent_ref[b, :HEAD_ROWS, :].astype(f32)
        loss = loss + sent_ref[b, HEAD_ROWS:, :].astype(f32)
    loss = jnp.sum(loss, axis=0, keepdims=True)
    pieces = jnp.concatenate(list(split3(loss)) + [jnp.zeros((13, 128), f32)], 0).astype(bf16)
    out_ref[:HEAD_ROWS, :] = grad.astype(bf16)
    out_ref[HEAD_ROWS:, :] = pieces


def total_kernel(me_ref, *refs):
    *shared_refs, grad_ref, loss_ref, all_ref = refs
    for k, ref in enumerate(shared_refs):
        all_ref[(me_ref[0] + MEMBERS - k) % MEMBERS] = ref[...]
    grad = jnp.zeros((HEAD_ROWS, CH), f32)
    loss = jnp.zeros((16, 128), f32)
    for j in range(MEMBERS):
        grad = grad + all_ref[j, :HEAD_ROWS, :].astype(f32)
        loss = loss + all_ref[j, HEAD_ROWS:, :].astype(f32)
    grad_ref[...] = grad
    loss_ref[...] = jnp.sum(jnp.sum(loss, axis=0, keepdims=True), axis=1, keepdims=True)


def backward_kernel(
    counts_ref, inverse_ref, q_ref, g_ref, kv_ref, kt_ref, mixed_hbm, p_hbm, out_hbm,
    off_ref, mixed_ref, acc_ref, dq_ref, dkv_ref,
    both0, both1, up0, up1, inner0, inner1, p0, p1, dq0, dq1, sems, p_sems, out_sems,
):
    blocks = BANDS
    boths, ups, inners, p_refs, dqs = (both0, both1), (up0, up1), (inner0, inner1), (p0, p1), (dq0, dq1)

    def copy(k, slot):
        return pltpu.make_async_copy(p_hbm.at[k], p_refs[slot], p_sems.at[slot])

    wait = fetch([(mixed_hbm, mixed_ref)], sems)
    copy(0, 0).start()
    copy(1, 1).start()
    offsets(counts_ref, off_ref)
    acc_ref[...] = jnp.zeros((ROWS, 128), f32)
    low = low_lanes(CAP)

    def prepare(k, slot):
        q = unfold(q_ref[k])
        g = unfold(g_ref[k])
        mixed = unfold(mixed_ref[k])
        inner = jnp.sum(jnp.where(low, g * mixed, 0.0).T, axis=0, keepdims=True)
        inners[slot][...] = jnp.broadcast_to(inner, (8, CAP))
        boths[slot][:CAP, :] = jnp.where(low, q, 0.0).astype(bf16)
        g = jnp.where(low, 0.0, swap(g))
        boths[slot][CAP:, :] = g.astype(bf16)
        ups[slot][...] = g.T.astype(bf16)

    def finish(k, slot):
        dq_ref[k] = refold((dqs[slot][...] * 0.125).T).astype(bf16)

    wait(1)
    prepare(0, 0)

    def step(k, j):
        other = 1 - j
        copy(k, j).wait()
        start, _ = window(off_ref, k)
        inner = inners[j][0:1, :]
        inverse = inverse_ref[pl.ds(k, 1), :]
        dq = None
        for first, size in CHUNKS:
            span = pl.ds(pl.multiple_of(start + first, 128), size)
            p = p_refs[j][first : first + size, :].astype(f32) * inverse
            ds = (p * (dot(kv_ref[span, :], ups[j][...]) - inner)).astype(bf16)
            acc_ref[span, :] += dot(jnp.concatenate([ds, p.astype(bf16)], 1), boths[j][...])
            part = dot(kt_ref[:, span], ds)
            dq = part if dq is None else dq + part
        dqs[j][...] = dq
        prepare(jnp.minimum(k + 1, blocks - 1), other)
        finish(jnp.maximum(k - 1, 0), other)

        @pl.when(k < blocks - 2)
        def _():
            copy(k + 2, j).start()

    by_two(blocks, step)
    finish(blocks - 1, 1)
    out_dq = pltpu.make_async_copy(dq_ref, out_hbm.at[:, pl.ds(0, 128), :], out_sems.at[0])
    out_dq.start()
    sub = lax.broadcasted_iota(jnp.int32, (1, 8, 128), 1)
    row = lax.broadcasted_iota(jnp.int32, (CAP, 128), 0)

    def give(b, carry):
        off = off_ref[b]
        shift = off & 7
        x = acc_ref[pl.ds(pl.multiple_of(off - shift + R, 8), 264), :].reshape(33, 8, 128)
        turned = pltpu.roll(x, (8 - shift) & 7, axis=1)
        x = jnp.where(sub + shift < 8, turned[:32], turned[1:]).reshape(CAP, 128)
        dkv_ref[b] = jnp.where(row < counts_ref[b], x, 0.0).astype(bf16)
        return carry

    some = BANDS // 4
    out_dkv = []
    for i in range(4):
        lax.fori_loop(i * some, (i + 1) * some, give, 0)
        bands = pl.ds(i * some, some)
        out_dkv.append(
            pltpu.make_async_copy(
                dkv_ref.at[bands], out_hbm.at[bands, pl.ds(128, CAP), :], out_sems.at[1 + i]
            )
        )
        out_dkv[-1].start()
    for out in [out_dq, *out_dkv]:
        out.wait()


def latent_kernel(
    d_ref, gain_ref, wq_hbm, wk_hbm, wv_hbm, lat_hbm, grad_hbm, out_ref,
    wq_ref, wk_ref, wv_ref, lat_ref, grad_ref, dq_ref, dk_ref, dv_ref, sems,
):
    wait = fetch(
        [(wq_hbm, wq_ref), (wk_hbm, wk_ref), (wv_hbm, wv_ref), (lat_hbm, lat_ref), (grad_hbm, grad_ref)],
        sems,
    )
    low = low_lanes(CAP)
    unfold_heads(parts(d_ref, 2), dq_ref)
    for pair in range(HEADS // 2):
        cols = slice(pair * 128, pair * 128 + 128)
        first = d_ref[2 * pair, 128:, :].astype(f32)
        second = d_ref[2 * pair + 1, 128:, :].astype(f32)
        dk_ref[:, cols] = jnp.where(low, first, swap(second)).astype(bf16)
        dv_ref[:, cols] = jnp.where(low, swap(first), second).astype(bf16)
    wait(1)
    normed = dot(dq_ref[...], wq_ref[...])
    wait(1)
    normed = normed + dot(dk_ref[...], wk_ref[...])
    wait(1)
    normed = normed + dot(dv_ref[...], wv_ref[...])
    wait(2)
    x = lat_ref[...].astype(f32)
    out = norm_backward(x, inverse_rms(x), normed * gain_ref[...])
    out_ref[...] = (grad_ref[...] + out).astype(bf16)


VMEM_MIB = dict(project=20, turn=20, forward=24, head=12, loss=20, share=8, total=8, latent=24, backward=24, grad_head=12)


def call(name, kernel, outs, scalars, arrays, held=(), held_out=(), scratch=(), sems=()):
    vmem = pl.BlockSpec(memory_space=pltpu.VMEM)
    smem = pl.BlockSpec(memory_space=pltpu.SMEM)
    hbm = pl.BlockSpec(memory_space=pltpu.HBM)
    return pl.pallas_call(
        kernel,
        out_shape=tuple(jax.ShapeDtypeStruct(s, d) for s, d in outs)
        + tuple(pltpu.HBM(s, d) for s, d in held_out),
        in_specs=[smem] * len(scalars) + [vmem] * len(arrays) + [hbm] * len(held),
        out_specs=(vmem,) * len(outs) + (hbm,) * len(held_out),
        scratch_shapes=[s if not isinstance(s, tuple) else pltpu.VMEM(*s) for s in scratch]
        + [pltpu.SemaphoreType.DMA((n,)) for n in sems],
        compiler_params=pltpu.CompilerParams(
            vmem_limit_bytes=VMEM_MIB[name] << 20 if name in VMEM_MIB else None
        ),
    )(*scalars, *arrays, *(pltpu.with_memory_space_constraint(a, pltpu.HBM) for a in held))


def exchange(x, axis):
    return lax.all_to_all(x, axis, split_axis=0, concat_axis=0, tiled=True)


def body(
    latent, observed, area_weight, counts, gain_attn, w_query, w_key, w_value, w_out, gain_head, w_head
):
    _, cap, width = latent.shape
    lat = latent.reshape(cap, width)
    gain_a = gain_attn.reshape(1, width)
    gain_h = gain_head.reshape(1, width)
    area = area_weight.reshape(2, 128)
    weight = ((width, width), bf16)
    offs = pltpu.SMEM((BANDS + 1,), jnp.int32)
    (x,) = call(
        "project",
        project_kernel,
        [((HEADS, 384, 128), bf16)],
        [],
        [],
        [gain_a, lat, w_query, w_key, w_value],
        scratch=[((1, width), f32), ((cap, width), bf16)] + [weight] * 3,
        sems=[5],
    )
    x, *weights = lax.optimization_barrier((x, w_head, w_out, w_query, w_key, w_value))
    turned = call(
        "turn",
        turn_kernel,
        [((CH, width), bf16), weight],
        [],
        [],
        weights,
        [weight] * 3,
        [((width, CH), bf16)] + [weight] * 5,
        [5],
    )
    x = exchange(x, "band")
    packed = ((BANDS, 128, 128), bf16)
    acc = ((ROWS, 128), f32)
    run = ((WIDTH, CAP), bf16)
    mixed, inverse, probs, kv, kt, q, own = call(
        "forward",
        forward_kernel,
        [packed, ((BANDS, CAP), f32)],
        [counts],
        [x],
        [],
        [((BANDS, WIDTH, CAP), bf16), ((ROWS, 128), bf16), ((HEAD, ROWS), bf16), packed, packed],
        [offs, ((ROWS, 128), bf16), ((ROWS, 128), bf16), ((TURNED, ROWS), bf16), acc]
        + [((256, CAP), bf16)] * 2
        + [run] * 2
        + [((TURNED - HEAD, CAP), f32)] * 2,
        [3, 2],
    )
    mixed = exchange(mixed, "band")
    hidden, predicted = call(
        "head",
        head_kernel,
        [],
        [],
        [mixed, w_out, gain_h, w_head],
        [lat],
        [((cap, width), f32), ((MEMBERS, cap, CH), bf16)],
        [((cap, width), bf16)] * 2 + [((cap, width), f32), ((cap, CH), bf16)],
        sems=[1, 4, MEMBERS],
    )
    predicted = exchange(predicted, "member")
    grad_pred, loss, grad_hidden, g = call(
        "loss",
        loss_kernel,
        [((cap, CH), bf16), ((8, 128), f32)],
        [counts],
        [predicted, area, observed, gain_h, turned[0], turned[1]],
        [hidden],
        [((cap, width), f32), packed],
        [((cap, width), f32)] * 2 + [packed],
        [1, 1],
    )
    (sent,) = call(
        "grad_head",
        grad_head_kernel,
        [((BANDS, HEAD_ROWS + 16, 128), bf16)],
        [],
        [grad_pred, loss, gain_h],
        [hidden],
        scratch=[((cap, width), f32)],
        sems=[1],
    )
    g = exchange(g, "band")
    g, sent = lax.optimization_barrier((g, sent))
    sent = exchange(sent, "band")
    (d,) = call(
        "backward",
        backward_kernel,
        [],
        [counts],
        [inverse, q, g, kv, kt],
        [own, probs],
        [((BANDS, 384, 128), bf16)],
        [offs, packed, acc, packed, ((BANDS, CAP, 128), bf16)]
        + [((2 * CAP, 128), bf16)] * 2
        + [((128, CAP), bf16)] * 2
        + [((8, CAP), f32)] * 2
        + [run] * 2
        + [((HEAD, CAP), f32)] * 2,
        [1, 2, 5],
    )
    d, sent = lax.optimization_barrier((d, sent))
    d = exchange(d, "band")
    (share,) = call("share", share_kernel, [((HEAD_ROWS + 16, 128), bf16)], [], [sent])
    shared = [share]
    for k in range(1, MEMBERS):
        shared.append(lax.ppermute(share, "member", [(j, (j + k) % MEMBERS) for j in range(MEMBERS)]))
    me = lax.axis_index("member").astype(jnp.int32).reshape(1)
    grad_head, loss = call(
        "total",
        total_kernel,
        [((HEAD_ROWS, CH), f32), ((1, 1), f32)],
        [me],
        shared,
        scratch=[((MEMBERS, HEAD_ROWS + 16, 128), bf16)],
    )
    (grad_latent,) = call(
        "latent",
        latent_kernel,
        [((cap, width), bf16)],
        [],
        [d, gain_a],
        [turned[2], turned[3], turned[4], lat, grad_hidden],
        scratch=[weight] * 3
        + [((cap, width), bf16), ((cap, width), f32)]
        + [((cap, width), bf16)] * 3,
        sems=[5],
    )
    return grad_latent.reshape(latent.shape), grad_head, loss.reshape(())


def solution(mesh):
    rows = P("member", "band", None)
    placed = (rows, P("band", None), P("band")) + (P(),) * 8
    return jax.shard_map(
        body,
        mesh=mesh,
        in_specs=placed,
        out_specs=(rows, P("band", None), P()),
        check_vma=False,
    )
```

```python
import jax
import jax.numpy as jnp
from jax import lax
from jax.experimental import pallas as pl
from jax.experimental.pallas import tpu as pltpu
from jax.sharding import PartitionSpec as P


HEADS = 16
HEAD = 64
CH = 128
R = 512
CAP = 256
MEMBERS = 8
BANDS = 16
LOG2E = 1.4426950408889634
EPS = 1e-06
SMOOTH = 0.0625
FAIR = 1.0 - 0.05 / MEMBERS
PAIR_SCALE = FAIR / (MEMBERS * (MEMBERS - 1.0))

HALF = CAP // 2
WIDTH = 2 * R + CAP + 128
ROWS = BANDS * CAP - CAP + WIDTH
EDGE = CAP + 128
CHUNKS = ((0, 512), (512, 512), (1024, 384))
BACK_CHUNKS = ((0, 768), (768, 640))
TURNED = 144
DEAD = -32768.0
UNROLL = 2
HEAD_ROWS = 64

f32 = jnp.float32
bf16 = jnp.bfloat16


def dot(a, b):
    return lax.dot_general(a, b, (((1,), (0,)), ((), ())), preferred_element_type=f32)


def dot_tn(a, b):
    return lax.dot_general(a, b, (((0,), (0,)), ((), ())), preferred_element_type=f32)


def swap(x):
    return pltpu.roll(x, HEAD, axis=1)


def low_lanes(rows):
    return lax.broadcasted_iota(jnp.int32, (rows, 128), 1) < HEAD


def fold(first, second):
    low = low_lanes(64)
    return jnp.where(low, first, swap(second)), jnp.where(low, swap(first), second)


def unfold(packed):
    packed = packed.astype(f32)
    other = swap(packed)
    return jnp.concatenate([packed[:64], other[:64], packed[64:], other[64:]], 0)


def refold(rows):
    return jnp.concatenate(
        [jnp.concatenate([rows[i : i + 64], rows[i + 64 : i + 128]], 1) for i in (0, 128)], 0
    )


def split3(x):
    high = x.astype(bf16).astype(f32)
    middle = (x - high).astype(bf16).astype(f32)
    return high, middle, (x - high - middle).astype(bf16).astype(f32)


def inverse_rms(x):
    return lax.rsqrt(jnp.mean(x * x, axis=-1, keepdims=True) + EPS)


def norm_backward(x, inverse, scaled):
    return inverse * scaled - x * (inverse * inverse * inverse) * jnp.mean(
        x * scaled, axis=-1, keepdims=True
    )


def fetch(copies, sems):
    started = [pltpu.make_async_copy(a, b, sems.at[i]) for i, (a, b) in enumerate(copies)]
    for copy in started:
        copy.start()

    def wait(count):
        for _ in range(count):
            started.pop(0).wait()

    return wait


def project_kernel(
    gain_hbm, lat_hbm, wq_hbm, wk_hbm, wv_hbm, out_ref, gain_ref, lat_ref, wq_ref, wk_ref, wv_ref, sems
):
    wait = fetch(
        [(gain_hbm, gain_ref), (lat_hbm, lat_ref), (wk_hbm, wk_ref), (wv_hbm, wv_ref), (wq_hbm, wq_ref)], sems
    )
    wait(2)
    x = lat_ref[...].astype(f32)
    normed = (x * inverse_rms(x) * gain_ref[...]).astype(bf16)
    low = low_lanes(CAP)
    wait(2)
    for quad in range(4):
        cols = slice(quad * 256, quad * 256 + 256)
        k = dot(normed, wk_ref[:, cols])
        v = dot(normed, wv_ref[:, cols])
        for half in range(2):
            head = quad * 4 + half * 2
            part = slice(half * 128, half * 128 + 128)
            kp, vp = k[:, part], v[:, part]
            out_ref[head, 128:, :] = jnp.where(low, kp, swap(vp)).astype(bf16)
            out_ref[head + 1, 128:, :] = jnp.where(low, swap(kp), vp).astype(bf16)
    wait(1)
    fold_heads(dot(normed, wq_ref[...]) * 0.125, parts(out_ref, 2))


def fold_heads(x, refs):
    for i, ref in enumerate(refs):
        for pair in range(HEADS // 2):
            part = x[i * HALF : (i + 1) * HALF, pair * 128 : pair * 128 + 128]
            first, second = fold(part[:64], part[64:])
            ref[2 * pair, 0:64, :] = first.astype(bf16)
            ref[2 * pair + 1, 0:64, :] = second.astype(bf16)


def unfold_heads(refs, rows_ref):
    for i, ref in enumerate(refs):
        for pair in range(HEADS // 2):
            first, second = fold(ref[2 * pair, 0:64, :].astype(f32), ref[2 * pair + 1, 0:64, :].astype(f32))
            cols = slice(pair * 128, pair * 128 + 128)
            rows_ref[i * HALF : i * HALF + 64, cols] = first.astype(bf16)
            rows_ref[i * HALF + 64 : (i + 1) * HALF, cols] = second.astype(bf16)


def parts(ref, n):
    return [ref.at[:, i * 64 : i * 64 + 64, :] for i in range(n)]


def turn_kernel(*refs):
    n = (len(refs) - 2) // 3
    w_hbm, outs, w_refs = refs[:n], refs[n : 2 * n], refs[2 * n : 3 * n]
    turned_ref, sems = refs[3 * n :]
    wait = fetch(list(zip(w_hbm, w_refs)), sems)
    for k, (w_ref, out) in enumerate(zip(w_refs, outs)):
        wait(1)
        rows = w_ref.shape[0]
        to = out if k < 2 else turned_ref
        for i in range(0, rows, 128):
            to[:, i : i + 128] = w_ref[i : i + 128, :].astype(f32).T.astype(bf16)
        if k >= 2:
            fetch([(turned_ref, out)], sems)(1)


def offsets(counts_ref, off_ref):
    def step(b, off):
        off_ref[b] = off
        return off + counts_ref[b]

    total = lax.fori_loop(0, BANDS, step, jnp.int32(0))
    off_ref[BANDS] = total
    return total


def compact(counts_ref, off_ref, x_ref, total, kv_ref, side_ref, kvt_ref, rows_ref):
    sub = lax.broadcasted_iota(jnp.int32, (1, 8, 128), 1)
    row = lax.broadcasted_iota(jnp.int32, (CAP, 128), 0)
    tail = R + BANDS * HALF
    rows_ref[tail:, :] = jnp.zeros((ROWS - tail, 128), f32)

    def place(b, carry):
        off = off_ref[b]
        shift = off & 7
        base = pl.multiple_of(off - shift + R, 8)
        x = jnp.where(row < counts_ref[b], x_ref[b, 128:, :].astype(f32), 0.0)
        turned = pltpu.roll(x.reshape(32, 8, 128), shift, axis=1)
        before = rows_ref[pl.ds(base, 8), :].reshape(1, 8, 128)
        shifted = jnp.concatenate([before, turned], 0)
        turned = jnp.concatenate([turned, jnp.zeros((1, 8, 128), f32)], 0)
        rows_ref[pl.ds(base, 264), :] = jnp.where(sub < shift, shifted, turned).reshape(264, 128)
        return carry

    lax.fori_loop(0, BANDS, place, 0)
    kvt_ref[128:, :] = jnp.ones((TURNED - 128, ROWS), bf16)
    lane = lax.broadcasted_iota(jnp.int32, (128, 128), 1)
    none = jnp.where(lane == 0, DEAD, 0.0)
    tile_row = lax.broadcasted_iota(jnp.int32, (128, 128), 0)
    for t in range(ROWS // 128):
        span = slice(t * 128, t * 128 + 128)
        bias = none if t * 128 < R else jnp.where(tile_row >= total + (R - t * 128), none, 0.0)
        if R <= t * 128 < R + BANDS * CAP:
            tile = rows_ref[span, :]
            kv_ref[span, :] = tile.astype(bf16)
            side_ref[span, :] = jnp.where(lane < HEAD, bias, swap(tile)).astype(bf16)
            kvt_ref[:128, span] = tile.astype(bf16).T
        else:
            kv_ref[span, :] = jnp.zeros((128, 128), bf16)
            side_ref[span, :] = bias.astype(bf16)
            kvt_ref[:128, span] = jnp.zeros((128, 128), bf16)


def window(off_ref, k):
    off = off_ref[k]
    return pl.multiple_of(off - (off & 127), 128), off & 127


def masked(e, first, least):
    gap = lax.broadcasted_iota(jnp.int32, (EDGE, CAP), 0) - lax.broadcasted_iota(
        jnp.int32, (EDGE, CAP), 1
    )
    if first == 0:
        return jnp.concatenate([jnp.where(gap >= least, e[:EDGE], 0.0), e[EDGE:]], 0)
    return e if first < 2 * R else jnp.where(gap <= least, e, 0.0)


def by_two(count, step):
    def some(i, carry):
        for j in range(UNROLL):
            step(UNROLL * i + j, j % 2)
        return carry

    lax.fori_loop(0, count // UNROLL, some, 0)


def forward_kernel(counts_ref, x_ref, *refs):
    blocks = BANDS
    mixed_ref, inverse_ref, e_hbm, kv_hbm, kt_hbm, q_hbm, own_hbm = refs[:7]
    off_ref, kv_ref, side_ref, kvt_ref, rows_ref = refs[7:12]
    qx0, qx1, e0, e1, out0, out1, sems, e_sems, q_sems, own_sems = refs[-10:]
    qx, e_refs, outs = (qx0, qx1), (e0, e1), (out0, out1)
    q_ref = x_ref.at[:, pl.ds(0, 128), :]
    give_q = fetch([(q_ref, q_hbm)], q_sems)
    total = offsets(counts_ref, off_ref)
    compact(counts_ref, off_ref, x_ref, total, kv_ref, side_ref, kvt_ref, rows_ref)
    give = fetch([(kv_ref, kv_hbm), (kvt_ref.at[pl.ds(0, HEAD), :], kt_hbm)], sems)
    lane = lax.broadcasted_iota(jnp.int32, (CAP, 128), 1)
    low = lane < HEAD
    one = jnp.where(lane == 0, 1.0, 0.0)

    def prepare(k, slot):
        scaled = jnp.where(low, unfold(q_ref[k]), 0.0) * LOG2E
        high = scaled.astype(bf16).astype(f32)
        columns = jnp.concatenate([high, jnp.where(low, one, swap(scaled - high))], 1)
        qx[slot][...] = columns.T.astype(bf16)

    def copy(k, slot):
        return pltpu.make_async_copy(e_refs[slot], e_hbm.at[k], e_sems.at[slot])

    def finish(k, slot):
        out = outs[slot][...]
        inverse = 1.0 / out[HEAD : HEAD + 1, :]
        inverse_ref[pl.ds(k, 1), :] = inverse
        mixed_ref[k] = refold((out[:HEAD] * inverse).T).astype(bf16)

    def own(half):
        bands = pl.ds(half * (BANDS // 2), BANDS // 2)
        return pltpu.make_async_copy(mixed_ref.at[bands], own_hbm.at[bands], own_sems.at[half])

    prepare(0, 0)

    def step(k, j):
        other = 1 - j

        @pl.when(k == BANDS // 2 + 1)
        def _():
            own(0).start()

        @pl.when(k > 1)
        def _():
            copy(k - 2, j).wait()

        start, least = window(off_ref, k)
        out = None
        for first, size in CHUNKS:
            span = pl.ds(pl.multiple_of(start + first, 128), size)
            rows = jnp.concatenate([kv_ref[span, :], side_ref[span, :]], 1)
            e = masked(jnp.exp2(dot(rows, qx[j][...])), first, least)
            e_refs[j][first : first + size, :] = e.astype(bf16)
            part = dot(kvt_ref[HEAD:, span], e_refs[j][first : first + size, :])
            out = part if out is None else out + part
        outs[j][...] = out
        finish(jnp.maximum(k - 1, 0), other)
        prepare(jnp.minimum(k + 1, blocks - 1), other)
        copy(k, j).start()

    by_two(blocks, step)
    finish(blocks - 1, 1)
    own(1).start()
    give(2)
    give_q(1)
    copy(blocks - 2, 0).wait()
    copy(blocks - 1, 1).wait()
    own(0).wait()
    own(1).wait()


def head_kernel(
    mixed_ref, wo_ref, gain_ref, wh_ref, lat_hbm, hidden_hbm, pred_hbm,
    rows_ref, lat_ref, hidden_ref, pred_ref, sems, hidden_sems, pred_sems,
):
    wait = fetch([(lat_hbm, lat_ref)], sems)
    unfold_heads(parts(mixed_ref, 2), rows_ref)
    wait(1)
    gives = []
    for i in range(4):
        cols = pl.ds(i * 256, 256)
        hidden_ref[:, cols] = lat_ref[:, cols].astype(f32) + dot(rows_ref[...], wo_ref[:, cols])
        gives.append(
            pltpu.make_async_copy(hidden_ref.at[:, cols], hidden_hbm.at[:, cols], hidden_sems.at[i])
        )
        gives[-1].start()
    hidden = hidden_ref[...]
    head_in = (hidden * inverse_rms(hidden) * gain_ref[...]).astype(bf16)
    pred_ref[...] = dot(head_in, wh_ref[...]).astype(bf16)
    out = fetch([(pred_ref, pred_hbm.at[j]) for j in range(MEMBERS)], pred_sems)
    for give in gives:
        give.wait()
    out(MEMBERS)


def loss_kernel(
    counts_ref, pred_ref, area_ref, obs_ref, gain_ref, wh_ref, wo_ref, hidden_hbm,
    grad_pred_ref, loss_ref, grad_hbm, out_hbm, hidden_ref, grad_ref, out_ref, sems, out_sems,
):
    wait = fetch([(hidden_hbm, hidden_ref)], sems)
    me, band = lax.axis_index("member"), lax.axis_index("band")
    total = lax.fori_loop(0, BANDS, lambda b, t: t + counts_ref[b], jnp.int32(0))
    area = area_ref[...]
    weight = jnp.concatenate(
        [jnp.broadcast_to(area[i : i + 1, :], (128, 128)).T for i in range(2)], 0
    )
    row = lax.broadcasted_iota(jnp.int32, (CAP, CH), 0)
    weight = jnp.where(row < counts_ref[band], weight, 0.0) / (total.astype(f32) * CH)
    mine = pred_ref[me].astype(f32)

    def smooth(gap):
        square = gap * gap + SMOOTH
        inverse = lax.rsqrt(square)
        return square * inverse, gap * inverse

    size, slope = smooth(mine - obs_ref[...].astype(f32))
    pair_size = jnp.zeros((CAP, CH), f32)
    pair_slope = jnp.zeros((CAP, CH), f32)
    for k in range(MEMBERS):
        a, da = smooth(mine - pred_ref[k].astype(f32))
        pair_size = pair_size + jnp.where(me == k, 0.0, 1.0) * a
        pair_slope = pair_slope + da
    loss = jnp.sum(weight * (size / MEMBERS - (0.5 * PAIR_SCALE) * pair_size), axis=0, keepdims=True)
    grad_pred = (weight * (slope / MEMBERS - PAIR_SCALE * pair_slope)).astype(bf16)

    wait(1)
    hidden = hidden_ref[...]
    gain = gain_ref[...]
    inverse = inverse_rms(hidden)
    scaled = dot(grad_pred, wh_ref[...]) * gain
    grad_hidden = norm_backward(hidden, inverse, scaled)
    grad_ref[...] = grad_hidden
    give = fetch([(grad_ref, grad_hbm)], sems)
    fold_heads(dot(grad_hidden.astype(bf16), wo_ref[...]), parts(out_ref, 2))
    out = fetch([(out_ref, out_hbm)], out_sems)
    grad_pred_ref[...] = grad_pred
    loss_ref[...] = jnp.broadcast_to(loss, (8, 128))
    give(1)
    out(1)


def grad_head_kernel(grad_pred_ref, loss_ref, gain_ref, hidden_hbm, sent_ref, hidden_ref, sems):
    fetch([(hidden_hbm, hidden_ref)], sems)(1)
    hidden = hidden_ref[...]
    head_in = (hidden * inverse_rms(hidden) * gain_ref[...]).astype(bf16)
    grad_head = dot_tn(head_in, grad_pred_ref[...])
    pieces = jnp.concatenate(
        list(split3(loss_ref[0:1, :])) + [jnp.zeros((13, 128), f32)], 0
    ).astype(bf16)
    for b in range(BANDS):
        sent_ref[b, :HEAD_ROWS, :] = grad_head[b * HEAD_ROWS : (b + 1) * HEAD_ROWS].astype(bf16)
        sent_ref[b, HEAD_ROWS:, :] = pieces


def share_kernel(sent_ref, out_ref):
    grad = jnp.zeros((HEAD_ROWS, CH), f32)
    loss = jnp.zeros((16, 128), f32)
    for b in range(BANDS):
        grad = grad + sent_ref[b, :HEAD_ROWS, :].astype(f32)
        loss = loss + sent_ref[b, HEAD_ROWS:, :].astype(f32)
    loss = jnp.sum(loss, axis=0, keepdims=True)
    pieces = jnp.concatenate(list(split3(loss)) + [jnp.zeros((13, 128), f32)], 0).astype(bf16)
    out_ref[:HEAD_ROWS, :] = grad.astype(bf16)
    out_ref[HEAD_ROWS:, :] = pieces


def total_kernel(me_ref, *refs):
    *shared_refs, grad_ref, loss_ref, all_ref = refs
    for k, ref in enumerate(shared_refs):
        all_ref[(me_ref[0] + MEMBERS - k) % MEMBERS] = ref[...]
    grad = jnp.zeros((HEAD_ROWS, CH), f32)
    loss = jnp.zeros((16, 128), f32)
    for j in range(MEMBERS):
        grad = grad + all_ref[j, :HEAD_ROWS, :].astype(f32)
        loss = loss + all_ref[j, HEAD_ROWS:, :].astype(f32)
    grad_ref[...] = grad
    loss_ref[...] = jnp.sum(jnp.sum(loss, axis=0, keepdims=True), axis=1, keepdims=True)


def backward_kernel(
    counts_ref, inverse_ref, q_ref, g_ref, kv_ref, kt_ref, mixed_hbm, p_hbm, out_hbm,
    off_ref, mixed_ref, acc_ref, dq_ref, dkv_ref,
    both0, both1, up0, up1, inner0, inner1, p0, p1, dq0, dq1, sems, p_sems, out_sems,
):
    blocks = BANDS
    boths, ups, inners, p_refs, dqs = (both0, both1), (up0, up1), (inner0, inner1), (p0, p1), (dq0, dq1)

    def copy(k, slot):
        return pltpu.make_async_copy(p_hbm.at[k], p_refs[slot], p_sems.at[slot])

    wait = fetch([(mixed_hbm, mixed_ref)], sems)
    copy(0, 0).start()
    copy(1, 1).start()
    offsets(counts_ref, off_ref)
    acc_ref[...] = jnp.zeros((ROWS, 128), f32)
    low = low_lanes(CAP)

    def prepare(k, slot):
        q = unfold(q_ref[k])
        g = unfold(g_ref[k])
        mixed = unfold(mixed_ref[k])
        inner = jnp.sum(jnp.where(low, g * mixed, 0.0).T, axis=0, keepdims=True)
        inners[slot][...] = jnp.broadcast_to(inner, (8, CAP))
        boths[slot][:CAP, :] = jnp.where(low, q, 0.0).astype(bf16)
        g = jnp.where(low, 0.0, swap(g))
        boths[slot][CAP:, :] = g.astype(bf16)
        ups[slot][...] = g.T.astype(bf16)

    def finish(k, slot):
        dq_ref[k] = refold((dqs[slot][...] * 0.125).T).astype(bf16)

    wait(1)
    prepare(0, 0)

    def step(k, j):
        other = 1 - j
        copy(k, j).wait()
        start, _ = window(off_ref, k)
        inner = inners[j][0:1, :]
        inverse = inverse_ref[pl.ds(k, 1), :]
        dq = None
        for first, size in BACK_CHUNKS:
            span = pl.ds(pl.multiple_of(start + first, 128), size)
            p = p_refs[j][first : first + size, :].astype(f32) * inverse
            ds = (p * (dot(kv_ref[span, :], ups[j][...]) - inner)).astype(bf16)
            acc_ref[span, :] += dot(ds, boths[j][:CAP, :]) + dot(p.astype(bf16), boths[j][CAP:, :])
            part = dot(kt_ref[:, span], ds)
            dq = part if dq is None else dq + part
        dqs[j][...] = dq
        prepare(jnp.minimum(k + 1, blocks - 1), other)
        finish(jnp.maximum(k - 1, 0), other)

        @pl.when(k < blocks - 2)
        def _():
            copy(k + 2, j).start()

    by_two(blocks, step)
    finish(blocks - 1, 1)
    out_dq = pltpu.make_async_copy(dq_ref, out_hbm.at[:, pl.ds(0, 128), :], out_sems.at[0])
    out_dq.start()
    sub = lax.broadcasted_iota(jnp.int32, (1, 8, 128), 1)
    row = lax.broadcasted_iota(jnp.int32, (CAP, 128), 0)

    def give(b, carry):
        off = off_ref[b]
        shift = off & 7
        x = acc_ref[pl.ds(pl.multiple_of(off - shift + R, 8), 264), :].reshape(33, 8, 128)
        turned = pltpu.roll(x, (8 - shift) & 7, axis=1)
        x = jnp.where(sub + shift < 8, turned[:32], turned[1:]).reshape(CAP, 128)
        dkv_ref[b] = jnp.where(row < counts_ref[b], x, 0.0).astype(bf16)
        return carry

    some = BANDS // 4
    out_dkv = []
    for i in range(4):
        lax.fori_loop(i * some, (i + 1) * some, give, 0)
        bands = pl.ds(i * some, some)
        out_dkv.append(
            pltpu.make_async_copy(
                dkv_ref.at[bands], out_hbm.at[bands, pl.ds(128, CAP), :], out_sems.at[1 + i]
            )
        )
        out_dkv[-1].start()
    for out in [out_dq, *out_dkv]:
        out.wait()


def latent_kernel(
    d_ref, gain_ref, wq_hbm, wk_hbm, wv_hbm, lat_hbm, grad_hbm, out_ref,
    wq_ref, wk_ref, wv_ref, lat_ref, grad_ref, dq_ref, dk_ref, dv_ref, sems,
):
    wait = fetch(
        [(wq_hbm, wq_ref), (wk_hbm, wk_ref), (wv_hbm, wv_ref), (lat_hbm, lat_ref), (grad_hbm, grad_ref)],
        sems,
    )
    low = low_lanes(CAP)
    unfold_heads(parts(d_ref, 2), dq_ref)
    for pair in range(HEADS // 2):
        cols = slice(pair * 128, pair * 128 + 128)
        first = d_ref[2 * pair, 128:, :].astype(f32)
        second = d_ref[2 * pair + 1, 128:, :].astype(f32)
        dk_ref[:, cols] = jnp.where(low, first, swap(second)).astype(bf16)
        dv_ref[:, cols] = jnp.where(low, swap(first), second).astype(bf16)
    wait(1)
    normed = dot(dq_ref[...], wq_ref[...])
    wait(1)
    normed = normed + dot(dk_ref[...], wk_ref[...])
    wait(1)
    normed = normed + dot(dv_ref[...], wv_ref[...])
    wait(2)
    x = lat_ref[...].astype(f32)
    out = norm_backward(x, inverse_rms(x), normed * gain_ref[...])
    out_ref[...] = (grad_ref[...] + out).astype(bf16)


VMEM_MIB = dict(project=20, turn=20, forward=24, head=12, loss=20, share=8, total=8, latent=24, backward=24, grad_head=12)


def call(name, kernel, outs, scalars, arrays, held=(), held_out=(), scratch=(), sems=()):
    vmem = pl.BlockSpec(memory_space=pltpu.VMEM)
    smem = pl.BlockSpec(memory_space=pltpu.SMEM)
    hbm = pl.BlockSpec(memory_space=pltpu.HBM)
    return pl.pallas_call(
        kernel,
        out_shape=tuple(jax.ShapeDtypeStruct(s, d) for s, d in outs)
        + tuple(pltpu.HBM(s, d) for s, d in held_out),
        in_specs=[smem] * len(scalars) + [vmem] * len(arrays) + [hbm] * len(held),
        out_specs=(vmem,) * len(outs) + (hbm,) * len(held_out),
        scratch_shapes=[s if not isinstance(s, tuple) else pltpu.VMEM(*s) for s in scratch]
        + [pltpu.SemaphoreType.DMA((n,)) for n in sems],
        compiler_params=pltpu.CompilerParams(
            vmem_limit_bytes=VMEM_MIB[name] << 20 if name in VMEM_MIB else None
        ),
    )(*scalars, *arrays, *(pltpu.with_memory_space_constraint(a, pltpu.HBM) for a in held))


def exchange(x, axis):
    return lax.all_to_all(x, axis, split_axis=0, concat_axis=0, tiled=True)


def body(
    latent, observed, area_weight, counts, gain_attn, w_query, w_key, w_value, w_out, gain_head, w_head
):
    _, cap, width = latent.shape
    lat = latent.reshape(cap, width)
    gain_a = gain_attn.reshape(1, width)
    gain_h = gain_head.reshape(1, width)
    area = area_weight.reshape(2, 128)
    weight = ((width, width), bf16)
    offs = pltpu.SMEM((BANDS + 1,), jnp.int32)
    (x,) = call(
        "project",
        project_kernel,
        [((HEADS, 384, 128), bf16)],
        [],
        [],
        [gain_a, lat, w_query, w_key, w_value],
        scratch=[((1, width), f32), ((cap, width), bf16)] + [weight] * 3,
        sems=[5],
    )
    x, *weights = lax.optimization_barrier((x, w_head, w_out, w_query, w_key, w_value))
    turned = call(
        "turn",
        turn_kernel,
        [((CH, width), bf16), weight],
        [],
        [],
        weights,
        [weight] * 3,
        [((width, CH), bf16)] + [weight] * 5,
        [5],
    )
    x = exchange(x, "band")
    packed = ((BANDS, 128, 128), bf16)
    acc = ((ROWS, 128), f32)
    run = ((WIDTH, CAP), bf16)
    mixed, inverse, probs, kv, kt, q, own = call(
        "forward",
        forward_kernel,
        [packed, ((BANDS, CAP), f32)],
        [counts],
        [x],
        [],
        [((BANDS, WIDTH, CAP), bf16), ((ROWS, 128), bf16), ((HEAD, ROWS), bf16), packed, packed],
        [offs, ((ROWS, 128), bf16), ((ROWS, 128), bf16), ((TURNED, ROWS), bf16), acc]
        + [((256, CAP), bf16)] * 2
        + [run] * 2
        + [((TURNED - HEAD, CAP), f32)] * 2,
        [2, 2, 1, 2],
    )
    mixed = exchange(mixed, "band")
    hidden, predicted = call(
        "head",
        head_kernel,
        [],
        [],
        [mixed, w_out, gain_h, w_head],
        [lat],
        [((cap, width), f32), ((MEMBERS, cap, CH), bf16)],
        [((cap, width), bf16)] * 2 + [((cap, width), f32), ((cap, CH), bf16)],
        sems=[1, 4, MEMBERS],
    )
    predicted = exchange(predicted, "member")
    grad_pred, loss, grad_hidden, g = call(
        "loss",
        loss_kernel,
        [((cap, CH), bf16), ((8, 128), f32)],
        [counts],
        [predicted, area, observed, gain_h, turned[0], turned[1]],
        [hidden],
        [((cap, width), f32), packed],
        [((cap, width), f32)] * 2 + [packed],
        [1, 1],
    )
    (sent,) = call(
        "grad_head",
        grad_head_kernel,
        [((BANDS, HEAD_ROWS + 16, 128), bf16)],
        [],
        [grad_pred, loss, gain_h],
        [hidden],
        scratch=[((cap, width), f32)],
        sems=[1],
    )
    g = exchange(g, "band")
    g, sent = lax.optimization_barrier((g, sent))
    sent = exchange(sent, "band")
    (d,) = call(
        "backward",
        backward_kernel,
        [],
        [counts],
        [inverse, q, g, kv, kt],
        [own, probs],
        [((BANDS, 384, 128), bf16)],
        [offs, packed, acc, packed, ((BANDS, CAP, 128), bf16)]
        + [((2 * CAP, 128), bf16)] * 2
        + [((128, CAP), bf16)] * 2
        + [((8, CAP), f32)] * 2
        + [run] * 2
        + [((HEAD, CAP), f32)] * 2,
        [1, 2, 5],
    )
    d, sent = lax.optimization_barrier((d, sent))
    d = exchange(d, "band")
    (share,) = call("share", share_kernel, [((HEAD_ROWS + 16, 128), bf16)], [], [sent])
    shared = [share]
    for k in range(1, MEMBERS):
        shared.append(lax.ppermute(share, "member", [(j, (j + k) % MEMBERS) for j in range(MEMBERS)]))
    me = lax.axis_index("member").astype(jnp.int32).reshape(1)
    grad_head, loss = call(
        "total",
        total_kernel,
        [((HEAD_ROWS, CH), f32), ((1, 1), f32)],
        [me],
        shared,
        scratch=[((MEMBERS, HEAD_ROWS + 16, 128), bf16)],
    )
    (grad_latent,) = call(
        "latent",
        latent_kernel,
        [((cap, width), bf16)],
        [],
        [d, gain_a],
        [turned[2], turned[3], turned[4], lat, grad_hidden],
        scratch=[weight] * 3
        + [((cap, width), bf16), ((cap, width), f32)]
        + [((cap, width), bf16)] * 3,
        sems=[5],
    )
    return grad_latent.reshape(latent.shape), grad_head, loss.reshape(())


def solution(mesh):
    rows = P("member", "band", None)
    placed = (rows, P("band", None), P("band")) + (P(),) * 8
    return jax.shard_map(
        body,
        mesh=mesh,
        in_specs=placed,
        out_specs=(rows, P("band", None), P()),
        check_vma=False,
    )
```

```python
import jax
import jax.numpy as jnp
from jax import lax
from jax.experimental import pallas as pl
from jax.experimental.pallas import tpu as pltpu
from jax.sharding import PartitionSpec as P


HEADS = 16
HEAD = 64
CH = 128
R = 512
CAP = 256
MEMBERS = 8
BANDS = 16
LOG2E = 1.4426950408889634
EPS = 1e-06
SMOOTH = 0.0625
FAIR = 1.0 - 0.05 / MEMBERS
PAIR_SCALE = FAIR / (MEMBERS * (MEMBERS - 1.0))

HALF = CAP // 2
WIDTH = 2 * R + CAP + 128
ROWS = BANDS * CAP - CAP + WIDTH
EDGE = CAP + 128
CHUNKS = ((0, 512), (512, 512), (1024, 384))
TURNED = 144
DEAD = -32768.0
UNROLL = 4
HEAD_ROWS = 64

f32 = jnp.float32
bf16 = jnp.bfloat16


def dot(a, b):
    return lax.dot_general(a, b, (((1,), (0,)), ((), ())), preferred_element_type=f32)


def dot_tn(a, b):
    return lax.dot_general(a, b, (((0,), (0,)), ((), ())), preferred_element_type=f32)


def swap(x):
    return pltpu.roll(x, HEAD, axis=1)


def low_lanes(rows):
    return lax.broadcasted_iota(jnp.int32, (rows, 128), 1) < HEAD


def fold(first, second):
    low = low_lanes(64)
    return jnp.where(low, first, swap(second)), jnp.where(low, swap(first), second)


def unfold(packed):
    packed = packed.astype(f32)
    other = swap(packed)
    return jnp.concatenate([packed[:64], other[:64], packed[64:], other[64:]], 0)


def refold(rows):
    return jnp.concatenate(
        [jnp.concatenate([rows[i : i + 64], rows[i + 64 : i + 128]], 1) for i in (0, 128)], 0
    )


def split3(x):
    high = x.astype(bf16).astype(f32)
    middle = (x - high).astype(bf16).astype(f32)
    return high, middle, (x - high - middle).astype(bf16).astype(f32)


def inverse_rms(x):
    return lax.rsqrt(jnp.mean(x * x, axis=-1, keepdims=True) + EPS)


def norm_backward(x, inverse, scaled):
    return inverse * scaled - x * (inverse * inverse * inverse) * jnp.mean(
        x * scaled, axis=-1, keepdims=True
    )


def fetch(copies, sems):
    started = [pltpu.make_async_copy(a, b, sems.at[i]) for i, (a, b) in enumerate(copies)]
    for copy in started:
        copy.start()

    def wait(count):
        for _ in range(count):
            started.pop(0).wait()

    return wait


def project_kernel(
    gain_hbm, lat_hbm, wq_hbm, wk_hbm, wv_hbm, out_ref, gain_ref, lat_ref, wq_ref, wk_ref, wv_ref, sems
):
    wait = fetch(
        [(gain_hbm, gain_ref), (lat_hbm, lat_ref), (wk_hbm, wk_ref), (wv_hbm, wv_ref), (wq_hbm, wq_ref)], sems
    )
    wait(2)
    x = lat_ref[...].astype(f32)
    normed = (x * inverse_rms(x) * gain_ref[...]).astype(bf16)
    low = low_lanes(CAP)
    wait(2)
    for quad in range(4):
        cols = slice(quad * 256, quad * 256 + 256)
        k = dot(normed, wk_ref[:, cols])
        v = dot(normed, wv_ref[:, cols])
        for half in range(2):
            head = quad * 4 + half * 2
            part = slice(half * 128, half * 128 + 128)
            kp, vp = k[:, part], v[:, part]
            out_ref[head, 128:, :] = jnp.where(low, kp, swap(vp)).astype(bf16)
            out_ref[head + 1, 128:, :] = jnp.where(low, swap(kp), vp).astype(bf16)
    wait(1)
    fold_heads(dot(normed, wq_ref[...]) * 0.125, parts(out_ref, 2))


def fold_heads(x, refs):
    for i, ref in enumerate(refs):
        for pair in range(HEADS // 2):
            part = x[i * HALF : (i + 1) * HALF, pair * 128 : pair * 128 + 128]
            first, second = fold(part[:64], part[64:])
            ref[2 * pair, 0:64, :] = first.astype(bf16)
            ref[2 * pair + 1, 0:64, :] = second.astype(bf16)


def unfold_heads(refs, rows_ref):
    for i, ref in enumerate(refs):
        for pair in range(HEADS // 2):
            first, second = fold(ref[2 * pair, 0:64, :].astype(f32), ref[2 * pair + 1, 0:64, :].astype(f32))
            cols = slice(pair * 128, pair * 128 + 128)
            rows_ref[i * HALF : i * HALF + 64, cols] = first.astype(bf16)
            rows_ref[i * HALF + 64 : (i + 1) * HALF, cols] = second.astype(bf16)


def parts(ref, n):
    return [ref.at[:, i * 64 : i * 64 + 64, :] for i in range(n)]


def turn_kernel(*refs):
    n = (len(refs) - 2) // 3
    w_hbm, outs, w_refs = refs[:n], refs[n : 2 * n], refs[2 * n : 3 * n]
    turned_ref, sems = refs[3 * n :]
    wait = fetch(list(zip(w_hbm, w_refs)), sems)
    for k, (w_ref, out) in enumerate(zip(w_refs, outs)):
        wait(1)
        rows = w_ref.shape[0]
        to = out if k < 2 else turned_ref
        for i in range(0, rows, 128):
            to[:, i : i + 128] = w_ref[i : i + 128, :].astype(f32).T.astype(bf16)
        if k >= 2:
            fetch([(turned_ref, out)], sems)(1)


def offsets(counts_ref, off_ref):
    def step(b, off):
        off_ref[b] = off
        return off + counts_ref[b]

    total = lax.fori_loop(0, BANDS, step, jnp.int32(0))
    off_ref[BANDS] = total
    return total


def compact(counts_ref, off_ref, x_ref, total, kv_ref, side_ref, kvt_ref, rows_ref):
    sub = lax.broadcasted_iota(jnp.int32, (1, 8, 128), 1)
    row = lax.broadcasted_iota(jnp.int32, (CAP, 128), 0)
    tail = R + BANDS * HALF
    rows_ref[tail:, :] = jnp.zeros((ROWS - tail, 128), f32)

    def place(b, carry):
        off = off_ref[b]
        shift = off & 7
        base = pl.multiple_of(off - shift + R, 8)
        x = jnp.where(row < counts_ref[b], x_ref[b, 128:, :].astype(f32), 0.0)
        turned = pltpu.roll(x.reshape(32, 8, 128), shift, axis=1)
        before = rows_ref[pl.ds(base, 8), :].reshape(1, 8, 128)
        shifted = jnp.concatenate([before, turned], 0)
        turned = jnp.concatenate([turned, jnp.zeros((1, 8, 128), f32)], 0)
        rows_ref[pl.ds(base, 264), :] = jnp.where(sub < shift, shifted, turned).reshape(264, 128)
        return carry

    lax.fori_loop(0, BANDS, place, 0)
    kvt_ref[128:, :] = jnp.ones((TURNED - 128, ROWS), bf16)
    lane = lax.broadcasted_iota(jnp.int32, (128, 128), 1)
    none = jnp.where(lane == 0, DEAD, 0.0)
    tile_row = lax.broadcasted_iota(jnp.int32, (128, 128), 0)
    for t in range(ROWS // 128):
        span = slice(t * 128, t * 128 + 128)
        bias = none if t * 128 < R else jnp.where(tile_row >= total + (R - t * 128), none, 0.0)
        if R <= t * 128 < R + BANDS * CAP:
            tile = rows_ref[span, :]
            kv_ref[span, :] = tile.astype(bf16)
            side_ref[span, :] = jnp.where(lane < HEAD, bias, swap(tile)).astype(bf16)
            kvt_ref[:128, span] = tile.astype(bf16).T
        else:
            kv_ref[span, :] = jnp.zeros((128, 128), bf16)
            side_ref[span, :] = bias.astype(bf16)
            kvt_ref[:128, span] = jnp.zeros((128, 128), bf16)


def window(off_ref, k):
    off = off_ref[k]
    return pl.multiple_of(off - (off & 127), 128), off & 127


def masked(e, first, least):
    gap = lax.broadcasted_iota(jnp.int32, (EDGE, CAP), 0) - lax.broadcasted_iota(
        jnp.int32, (EDGE, CAP), 1
    )
    if first == 0:
        return jnp.concatenate([jnp.where(gap >= least, e[:EDGE], 0.0), e[EDGE:]], 0)
    return e if first < 2 * R else jnp.where(gap <= least, e, 0.0)


def by_two(count, step):
    def some(i, carry):
        for j in range(UNROLL):
            step(UNROLL * i + j, j % 2)
        return carry

    lax.fori_loop(0, count // UNROLL, some, 0)


def forward_kernel(counts_ref, x_ref, *refs):
    blocks = BANDS
    mixed_ref, inverse_ref, e_hbm, kv_hbm, kt_hbm, q_hbm, own_hbm = refs[:7]
    off_ref, kv_ref, side_ref, kvt_ref, rows_ref = refs[7:12]
    qx0, qx1, e0, e1, out0, out1, sems, e_sems, q_sems, own_sems = refs[-10:]
    qx, e_refs, outs = (qx0, qx1), (e0, e1), (out0, out1)
    q_ref = x_ref.at[:, pl.ds(0, 128), :]
    give_q = fetch([(q_ref, q_hbm)], q_sems)
    total = offsets(counts_ref, off_ref)
    compact(counts_ref, off_ref, x_ref, total, kv_ref, side_ref, kvt_ref, rows_ref)
    give = fetch([(kv_ref, kv_hbm), (kvt_ref.at[pl.ds(0, HEAD), :], kt_hbm)], sems)
    lane = lax.broadcasted_iota(jnp.int32, (CAP, 128), 1)
    low = lane < HEAD
    one = jnp.where(lane == 0, 1.0, 0.0)

    def prepare(k, slot):
        scaled = jnp.where(low, unfold(q_ref[k]), 0.0) * LOG2E
        high = scaled.astype(bf16).astype(f32)
        columns = jnp.concatenate([high, jnp.where(low, one, swap(scaled - high))], 1)
        qx[slot][...] = columns.T.astype(bf16)

    def copy(k, slot):
        return pltpu.make_async_copy(e_refs[slot], e_hbm.at[k], e_sems.at[slot])

    def finish(k, slot):
        out = outs[slot][...]
        inverse = 1.0 / out[HEAD : HEAD + 1, :]
        inverse_ref[pl.ds(k, 1), :] = inverse
        mixed_ref[k] = refold((out[:HEAD] * inverse).T).astype(bf16)

    def own(half):
        bands = pl.ds(half * (BANDS // 2), BANDS // 2)
        return pltpu.make_async_copy(mixed_ref.at[bands], own_hbm.at[bands], own_sems.at[half])

    prepare(0, 0)

    def step(k, j):
        other = 1 - j

        @pl.when(k == BANDS // 2 + 1)
        def _():
            own(0).start()

        @pl.when(k > 1)
        def _():
            copy(k - 2, j).wait()

        start, least = window(off_ref, k)
        out = None
        for first, size in CHUNKS:
            span = pl.ds(pl.multiple_of(start + first, 128), size)
            rows = jnp.concatenate([kv_ref[span, :], side_ref[span, :]], 1)
            e = masked(jnp.exp2(dot(rows, qx[j][...])), first, least)
            e_refs[j][first : first + size, :] = e.astype(bf16)
            part = dot(kvt_ref[HEAD:, span], e_refs[j][first : first + size, :])
            out = part if out is None else out + part
        outs[j][...] = out
        finish(jnp.maximum(k - 1, 0), other)
        prepare(jnp.minimum(k + 1, blocks - 1), other)
        copy(k, j).start()

    by_two(blocks, step)
    finish(blocks - 1, 1)
    own(1).start()
    give(2)
    give_q(1)
    copy(blocks - 2, 0).wait()
    copy(blocks - 1, 1).wait()
    own(0).wait()
    own(1).wait()


def head_kernel(
    mixed_ref, wo_ref, gain_ref, wh_ref, lat_hbm, hidden_hbm, pred_hbm,
    rows_ref, lat_ref, hidden_ref, pred_ref, sems, hidden_sems, pred_sems,
):
    wait = fetch([(lat_hbm, lat_ref)], sems)
    unfold_heads(parts(mixed_ref, 2), rows_ref)
    wait(1)
    gives = []
    for i in range(4):
        cols = pl.ds(i * 256, 256)
        hidden_ref[:, cols] = lat_ref[:, cols].astype(f32) + dot(rows_ref[...], wo_ref[:, cols])
        gives.append(
            pltpu.make_async_copy(hidden_ref.at[:, cols], hidden_hbm.at[:, cols], hidden_sems.at[i])
        )
        gives[-1].start()
    hidden = hidden_ref[...]
    head_in = (hidden * inverse_rms(hidden) * gain_ref[...]).astype(bf16)
    pred_ref[...] = dot(head_in, wh_ref[...]).astype(bf16)
    out = fetch([(pred_ref, pred_hbm.at[j]) for j in range(MEMBERS)], pred_sems)
    for give in gives:
        give.wait()
    out(MEMBERS)


def loss_kernel(
    counts_ref, pred_ref, area_ref, obs_ref, gain_ref, wh_ref, wo_ref, hidden_hbm,
    grad_pred_ref, loss_ref, grad_hbm, out_hbm, hidden_ref, grad_ref, out_ref, sems, out_sems,
):
    wait = fetch([(hidden_hbm, hidden_ref)], sems)
    me, band = lax.axis_index("member"), lax.axis_index("band")
    total = lax.fori_loop(0, BANDS, lambda b, t: t + counts_ref[b], jnp.int32(0))
    area = area_ref[...]
    weight = jnp.concatenate(
        [jnp.broadcast_to(area[i : i + 1, :], (128, 128)).T for i in range(2)], 0
    )
    row = lax.broadcasted_iota(jnp.int32, (CAP, CH), 0)
    weight = jnp.where(row < counts_ref[band], weight, 0.0) / (total.astype(f32) * CH)
    mine = pred_ref[me].astype(f32)

    def smooth(gap):
        square = gap * gap + SMOOTH
        inverse = lax.rsqrt(square)
        return square * inverse, gap * inverse

    size, slope = smooth(mine - obs_ref[...].astype(f32))
    pair_size = jnp.zeros((CAP, CH), f32)
    pair_slope = jnp.zeros((CAP, CH), f32)
    for k in range(MEMBERS):
        a, da = smooth(mine - pred_ref[k].astype(f32))
        pair_size = pair_size + jnp.where(me == k, 0.0, 1.0) * a
        pair_slope = pair_slope + da
    loss = jnp.sum(weight * (size / MEMBERS - (0.5 * PAIR_SCALE) * pair_size), axis=0, keepdims=True)
    grad_pred = (weight * (slope / MEMBERS - PAIR_SCALE * pair_slope)).astype(bf16)

    wait(1)
    hidden = hidden_ref[...]
    gain = gain_ref[...]
    inverse = inverse_rms(hidden)
    scaled = dot(grad_pred, wh_ref[...]) * gain
    grad_hidden = norm_backward(hidden, inverse, scaled)
    grad_ref[...] = grad_hidden
    give = fetch([(grad_ref, grad_hbm)], sems)
    fold_heads(dot(grad_hidden.astype(bf16), wo_ref[...]), parts(out_ref, 2))
    out = fetch([(out_ref, out_hbm)], out_sems)
    grad_pred_ref[...] = grad_pred
    loss_ref[...] = jnp.broadcast_to(loss, (8, 128))
    give(1)
    out(1)


def grad_head_kernel(grad_pred_ref, loss_ref, gain_ref, hidden_hbm, sent_ref, hidden_ref, sems):
    fetch([(hidden_hbm, hidden_ref)], sems)(1)
    hidden = hidden_ref[...]
    head_in = (hidden * inverse_rms(hidden) * gain_ref[...]).astype(bf16)
    grad_head = dot_tn(head_in, grad_pred_ref[...])
    pieces = jnp.concatenate(
        list(split3(loss_ref[0:1, :])) + [jnp.zeros((13, 128), f32)], 0
    ).astype(bf16)
    for b in range(BANDS):
        sent_ref[b, :HEAD_ROWS, :] = grad_head[b * HEAD_ROWS : (b + 1) * HEAD_ROWS].astype(bf16)
        sent_ref[b, HEAD_ROWS:, :] = pieces


def share_kernel(sent_ref, out_ref):
    grad = jnp.zeros((HEAD_ROWS, CH), f32)
    loss = jnp.zeros((16, 128), f32)
    for b in range(BANDS):
        grad = grad + sent_ref[b, :HEAD_ROWS, :].astype(f32)
        loss = loss + sent_ref[b, HEAD_ROWS:, :].astype(f32)
    loss = jnp.sum(loss, axis=0, keepdims=True)
    pieces = jnp.concatenate(list(split3(loss)) + [jnp.zeros((13, 128), f32)], 0).astype(bf16)
    out_ref[:HEAD_ROWS, :] = grad.astype(bf16)
    out_ref[HEAD_ROWS:, :] = pieces


def total_kernel(me_ref, *refs):
    *shared_refs, grad_ref, loss_ref, all_ref = refs
    for k, ref in enumerate(shared_refs):
        all_ref[(me_ref[0] + MEMBERS - k) % MEMBERS] = ref[...]
    grad = jnp.zeros((HEAD_ROWS, CH), f32)
    loss = jnp.zeros((16, 128), f32)
    for j in range(MEMBERS):
        grad = grad + all_ref[j, :HEAD_ROWS, :].astype(f32)
        loss = loss + all_ref[j, HEAD_ROWS:, :].astype(f32)
    grad_ref[...] = grad
    loss_ref[...] = jnp.sum(jnp.sum(loss, axis=0, keepdims=True), axis=1, keepdims=True)


def backward_kernel(
    counts_ref, inverse_ref, q_ref, g_ref, kv_ref, kt_ref, mixed_hbm, p_hbm, out_hbm,
    off_ref, mixed_ref, acc_ref, dq_ref, dkv_ref,
    both0, both1, up0, up1, inner0, inner1, p0, p1, dq0, dq1, sems, p_sems, out_sems,
):
    blocks = BANDS
    boths, ups, inners, p_refs, dqs = (both0, both1), (up0, up1), (inner0, inner1), (p0, p1), (dq0, dq1)

    def copy(k, slot):
        return pltpu.make_async_copy(p_hbm.at[k], p_refs[slot], p_sems.at[slot])

    wait = fetch([(mixed_hbm, mixed_ref)], sems)
    copy(0, 0).start()
    copy(1, 1).start()
    offsets(counts_ref, off_ref)
    acc_ref[...] = jnp.zeros((ROWS, 128), f32)
    low = low_lanes(CAP)

    def prepare(k, slot):
        q = unfold(q_ref[k])
        g = unfold(g_ref[k])
        mixed = unfold(mixed_ref[k])
        inner = jnp.sum(jnp.where(low, g * mixed, 0.0).T, axis=0, keepdims=True)
        inners[slot][...] = jnp.broadcast_to(inner, (8, CAP))
        boths[slot][:CAP, :] = jnp.where(low, q, 0.0).astype(bf16)
        g = jnp.where(low, 0.0, swap(g))
        boths[slot][CAP:, :] = g.astype(bf16)
        ups[slot][...] = g.T.astype(bf16)

    def finish(k, slot):
        dq_ref[k] = refold((dqs[slot][...] * 0.125).T).astype(bf16)

    wait(1)
    prepare(0, 0)

    def step(k, j):
        other = 1 - j
        copy(k, j).wait()
        start, _ = window(off_ref, k)
        inner = inners[j][0:1, :]
        inverse = inverse_ref[pl.ds(k, 1), :]
        dq = None
        for first, size in CHUNKS:
            span = pl.ds(pl.multiple_of(start + first, 128), size)
            p = p_refs[j][first : first + size, :].astype(f32) * inverse
            ds = (p * (dot(kv_ref[span, :], ups[j][...]) - inner)).astype(bf16)
            acc_ref[span, :] += dot(jnp.concatenate([ds, p.astype(bf16)], 1), boths[j][...])
            part = dot(kt_ref[:, span], ds)
            dq = part if dq is None else dq + part
        dqs[j][...] = dq
        prepare(jnp.minimum(k + 1, blocks - 1), other)
        finish(jnp.maximum(k - 1, 0), other)

        @pl.when(k < blocks - 2)
        def _():
            copy(k + 2, j).start()

    by_two(blocks, step)
    finish(blocks - 1, 1)
    out_dq = pltpu.make_async_copy(dq_ref, out_hbm.at[:, pl.ds(0, 128), :], out_sems.at[0])
    out_dq.start()
    sub = lax.broadcasted_iota(jnp.int32, (1, 8, 128), 1)
    row = lax.broadcasted_iota(jnp.int32, (CAP, 128), 0)

    def give(b, carry):
        off = off_ref[b]
        shift = off & 7
        x = acc_ref[pl.ds(pl.multiple_of(off - shift + R, 8), 264), :].reshape(33, 8, 128)
        turned = pltpu.roll(x, (8 - shift) & 7, axis=1)
        x = jnp.where(sub + shift < 8, turned[:32], turned[1:]).reshape(CAP, 128)
        dkv_ref[b] = jnp.where(row < counts_ref[b], x, 0.0).astype(bf16)
        return carry

    some = BANDS // 4
    out_dkv = []
    for i in range(4):
        lax.fori_loop(i * some, (i + 1) * some, give, 0)
        bands = pl.ds(i * some, some)
        out_dkv.append(
            pltpu.make_async_copy(
                dkv_ref.at[bands], out_hbm.at[bands, pl.ds(128, CAP), :], out_sems.at[1 + i]
            )
        )
        out_dkv[-1].start()
    for out in [out_dq, *out_dkv]:
        out.wait()


def latent_kernel(
    d_ref, gain_ref, wq_hbm, wk_hbm, wv_hbm, lat_hbm, grad_hbm, out_ref,
    wq_ref, wk_ref, wv_ref, lat_ref, grad_ref, dq_ref, dk_ref, dv_ref, sems,
):
    wait = fetch(
        [(wq_hbm, wq_ref), (wk_hbm, wk_ref), (wv_hbm, wv_ref), (lat_hbm, lat_ref), (grad_hbm, grad_ref)],
        sems,
    )
    low = low_lanes(CAP)
    unfold_heads(parts(d_ref, 2), dq_ref)
    for pair in range(HEADS // 2):
        cols = slice(pair * 128, pair * 128 + 128)
        first = d_ref[2 * pair, 128:, :].astype(f32)
        second = d_ref[2 * pair + 1, 128:, :].astype(f32)
        dk_ref[:, cols] = jnp.where(low, first, swap(second)).astype(bf16)
        dv_ref[:, cols] = jnp.where(low, swap(first), second).astype(bf16)
    wait(1)
    normed = dot(dq_ref[...], wq_ref[...])
    wait(1)
    normed = normed + dot(dk_ref[...], wk_ref[...])
    wait(1)
    normed = normed + dot(dv_ref[...], wv_ref[...])
    wait(2)
    x = lat_ref[...].astype(f32)
    out = norm_backward(x, inverse_rms(x), normed * gain_ref[...])
    out_ref[...] = (grad_ref[...] + out).astype(bf16)


VMEM_MIB = dict(project=20, turn=20, forward=24, head=12, loss=20, share=8, total=8, latent=24, backward=24, grad_head=12)


def call(name, kernel, outs, scalars, arrays, held=(), held_out=(), scratch=(), sems=()):
    vmem = pl.BlockSpec(memory_space=pltpu.VMEM)
    smem = pl.BlockSpec(memory_space=pltpu.SMEM)
    hbm = pl.BlockSpec(memory_space=pltpu.HBM)
    return pl.pallas_call(
        kernel,
        out_shape=tuple(jax.ShapeDtypeStruct(s, d) for s, d in outs)
        + tuple(pltpu.HBM(s, d) for s, d in held_out),
        in_specs=[smem] * len(scalars) + [vmem] * len(arrays) + [hbm] * len(held),
        out_specs=(vmem,) * len(outs) + (hbm,) * len(held_out),
        scratch_shapes=[s if not isinstance(s, tuple) else pltpu.VMEM(*s) for s in scratch]
        + [pltpu.SemaphoreType.DMA((n,)) for n in sems],
        compiler_params=pltpu.CompilerParams(
            vmem_limit_bytes=VMEM_MIB[name] << 20 if name in VMEM_MIB else None
        ),
    )(*scalars, *arrays, *(pltpu.with_memory_space_constraint(a, pltpu.HBM) for a in held))


def exchange(x, axis):
    return lax.all_to_all(x, axis, split_axis=0, concat_axis=0, tiled=True)


def body(
    latent, observed, area_weight, counts, gain_attn, w_query, w_key, w_value, w_out, gain_head, w_head
):
    _, cap, width = latent.shape
    lat = latent.reshape(cap, width)
    gain_a = gain_attn.reshape(1, width)
    gain_h = gain_head.reshape(1, width)
    area = area_weight.reshape(2, 128)
    weight = ((width, width), bf16)
    offs = pltpu.SMEM((BANDS + 1,), jnp.int32)
    (x,) = call(
        "project",
        project_kernel,
        [((HEADS, 384, 128), bf16)],
        [],
        [],
        [gain_a, lat, w_query, w_key, w_value],
        scratch=[((1, width), f32), ((cap, width), bf16)] + [weight] * 3,
        sems=[5],
    )
    x, *weights = lax.optimization_barrier((x, w_head, w_out, w_query, w_key, w_value))
    turned = call(
        "turn",
        turn_kernel,
        [((CH, width), bf16), weight],
        [],
        [],
        weights,
        [weight] * 3,
        [((width, CH), bf16)] + [weight] * 5,
        [5],
    )
    x = exchange(x, "band")
    packed = ((BANDS, 128, 128), bf16)
    acc = ((ROWS, 128), f32)
    run = ((WIDTH, CAP), bf16)
    mixed, inverse, probs, kv, kt, q, own = call(
        "forward",
        forward_kernel,
        [packed, ((BANDS, CAP), f32)],
        [counts],
        [x],
        [],
        [((BANDS, WIDTH, CAP), bf16), ((ROWS, 128), bf16), ((HEAD, ROWS), bf16), packed, packed],
        [offs, ((ROWS, 128), bf16), ((ROWS, 128), bf16), ((TURNED, ROWS), bf16), acc]
        + [((256, CAP), bf16)] * 2
        + [run] * 2
        + [((TURNED - HEAD, CAP), f32)] * 2,
        [2, 2, 1, 2],
    )
    mixed = exchange(mixed, "band")
    hidden, predicted = call(
        "head",
        head_kernel,
        [],
        [],
        [mixed, w_out, gain_h, w_head],
        [lat],
        [((cap, width), f32), ((MEMBERS, cap, CH), bf16)],
        [((cap, width), bf16)] * 2 + [((cap, width), f32), ((cap, CH), bf16)],
        sems=[1, 4, MEMBERS],
    )
    predicted = exchange(predicted, "member")
    grad_pred, loss, grad_hidden, g = call(
        "loss",
        loss_kernel,
        [((cap, CH), bf16), ((8, 128), f32)],
        [counts],
        [predicted, area, observed, gain_h, turned[0], turned[1]],
        [hidden],
        [((cap, width), f32), packed],
        [((cap, width), f32)] * 2 + [packed],
        [1, 1],
    )
    (sent,) = call(
        "grad_head",
        grad_head_kernel,
        [((BANDS, HEAD_ROWS + 16, 128), bf16)],
        [],
        [grad_pred, loss, gain_h],
        [hidden],
        scratch=[((cap, width), f32)],
        sems=[1],
    )
    g = exchange(g, "band")
    g, sent = lax.optimization_barrier((g, sent))
    sent = exchange(sent, "band")
    (d,) = call(
        "backward",
        backward_kernel,
        [],
        [counts],
        [inverse, q, g, kv, kt],
        [own, probs],
        [((BANDS, 384, 128), bf16)],
        [offs, packed, acc, packed, ((BANDS, CAP, 128), bf16)]
        + [((2 * CAP, 128), bf16)] * 2
        + [((128, CAP), bf16)] * 2
        + [((8, CAP), f32)] * 2
        + [run] * 2
        + [((HEAD, CAP), f32)] * 2,
        [1, 2, 5],
    )
    d, sent = lax.optimization_barrier((d, sent))
    d = exchange(d, "band")
    (share,) = call("share", share_kernel, [((HEAD_ROWS + 16, 128), bf16)], [], [sent])
    shared = [share]
    for k in range(1, MEMBERS):
        shared.append(lax.ppermute(share, "member", [(j, (j + k) % MEMBERS) for j in range(MEMBERS)]))
    me = lax.axis_index("member").astype(jnp.int32).reshape(1)
    grad_head, loss = call(
        "total",
        total_kernel,
        [((HEAD_ROWS, CH), f32), ((1, 1), f32)],
        [me],
        shared,
        scratch=[((MEMBERS, HEAD_ROWS + 16, 128), bf16)],
    )
    (grad_latent,) = call(
        "latent",
        latent_kernel,
        [((cap, width), bf16)],
        [],
        [d, gain_a],
        [turned[2], turned[3], turned[4], lat, grad_hidden],
        scratch=[weight] * 3
        + [((cap, width), bf16), ((cap, width), f32)]
        + [((cap, width), bf16)] * 3,
        sems=[5],
    )
    return grad_latent.reshape(latent.shape), grad_head, loss.reshape(())


def solution(mesh):
    rows = P("member", "band", None)
    placed = (rows, P("band", None), P("band")) + (P(),) * 8
    return jax.shard_map(
        body,
        mesh=mesh,
        in_specs=placed,
        out_specs=(rows, P("band", None), P()),
        check_vma=False,
    )
```
